32 devices in a mesh: dp: 8 (over z, x), ctx: 4 (over y, core).
Axes of the slice: x: 2, y: 2, z: 4, core: 2. Of those that a mesh axis runs over, the one named last changes fastest.
Arguments:
- block_input: bfloat16 [8, 512, 1024], P('dp', 'ctx'), may hold values from -6 to 6
- segment_ids: int32 [8, 512], P('dp'), may hold values from 0 to 2, never falling along the last dimension, each value on 1 to 320 neighbouring positions
- ln1_gain: bfloat16 [1024], P('dp'), may hold values from 0.25 to 1.75
- ln1_bias: bfloat16 [1024], P('dp'), may hold values from -3 to 3
- qkv_weight: bfloat16 [1024, 3, 1024], P('dp', None, 'ctx'), may hold values from -3 to 3
- query_bias: bfloat16 [1024], P('dp'), may hold values from -3 to 3
- value_bias: bfloat16 [1024], P('dp'), may hold values from -1.1953125 to 1.1953125
- proj_weight: bfloat16 [1024, 1024], P('ctx', 'dp'), may hold values from -0.75 to 0.75
- proj_bias: bfloat16 [1024], P('dp'), may hold values from -3 to 3
- ln2_gain: bfloat16 [1024], P('dp'), may hold values from 0.25 to 1.75
- ln2_bias: bfloat16 [1024], P('dp'), may hold values from -3 to 3
- fc_weight: bfloat16 [1024, 4096], P('dp', 'ctx'), may hold values from -0.1875 to 0.1875
- fc_bias: bfloat16 [4096], P('dp'), may hold values from -3 to 3
- out_weight: bfloat16 [4096, 1024], P('ctx', 'dp'), may hold values from -0.09375 to 0.09375
- out_bias: bfloat16 [1024], P('dp'), may hold values from -3 to 3
- cotangent: bfloat16 [8, 512, 1024], P('dp', 'ctx'), may hold values from -6 to 6
Outputs:
- block_output: bfloat16 [8, 512, 1024], P('dp', 'ctx')
- input_grad: float32 [8, 512, 1024], P('dp', 'ctx')
- ln1_gain_grad: float32 [1024], P('dp')
- ln1_bias_grad: float32 [1024], P('dp')
- qkv_weight_grad: float32 [1024, 3, 1024], P('dp', None, 'ctx')
- query_bias_grad: float32 [1024], P('dp')
- value_bias_grad: float32 [1024], P('dp')
- proj_weight_grad: float32 [1024, 1024], P('ctx', 'dp')
- proj_bias_grad: float32 [1024], P('dp')
- ln2_gain_grad: float32 [1024], P('dp')
- ln2_bias_grad: float32 [1024], P('dp')
- fc_weight_grad: float32 [1024, 4096], P('dp', 'ctx')
- fc_bias_grad: float32 [4096], P('dp')
- out_weight_grad: float32 [4096, 1024], P('ctx', 'dp')
- out_bias_grad: float32 [1024], P('dp')
The draws below stay inside these ranges and needn't reach their ends.
Inputs may be any that keep to these rules, and one draw needn't show every extreme that they name: `segment_ids`: segment numbers never fall along a sequence.
All inputs are finite; a program needn't handle non-finite values.
Results may differ from the reference program's by a relative error of at most 0.019.
Values may be sent and summed in bfloat16 or wider, within the bound.
A program may use at most 128 MiB of HBM per device.

```python
import math
import jax
import jax.numpy as jnp
import numpy as np
from jax import lax

D = 1024
HEADS = 16
HD = 64
FF = 4096
SEQ_LEN = 512
SEQS = 8


def draw_qkv_weight(key, part):
    normal_base = jax.random.normal(jax.random.fold_in(key, 11), (D, 3 * D), jnp.float32)
    return (jnp.clip(normal_base, -6.0, 6.0) / math.sqrt(D)).reshape(D, 3, D).astype(jnp.bfloat16)


def spiked(result, key, source, target, shards_of, factor):
    owner, partner = [(jnp.arange(result.shape[position]) // (result.shape[position] // shards_of)).reshape([-1 if axis == position else 1 for axis in range(result.ndim)]) for position in (source, target)]
    chosen = jax.random.permutation(key, shards_of)[partner]
    strong = (owner == chosen) | (owner == (partner + shards_of // 2) % shards_of)
    return jnp.where(strong, factor * result, result)


def block_levels(stream_key, shape, pieces, smallest, high):
    loudness, own = 1.0, jax.random.fold_in(stream_key, 6)
    for axis_at, shards_of in pieces:
        draws = jnp.exp(jax.random.uniform(jax.random.fold_in(own, axis_at), (shards_of,), jnp.float32, smallest / len(pieces), high / len(pieces)))
        loudness = loudness * jnp.repeat(draws, shape[axis_at] // shards_of).reshape([-1 if axis == axis_at else 1 for axis in range(len(shape))])
    return loudness


def profile(count, total, reach, lean):
    portions = [(1 << 20) // math.isqrt(standing ** lean) + 1 for standing in range(2, count + 1)]
    rest, counts = total - reach - (count - 1), [1] * (count - 1)
    while rest > 0:
        free = [i for i in range(count - 1) if counts[i] < reach]
        pool, remaining = sum([portions[i] for i in free]), rest
        for i in free:
            extra = min(reach - counts[i], max(1, remaining * portions[i] // pool), rest)
            counts[i] = counts[i] + extra
            rest = rest - extra
    return np.array([reach] + counts)


def uneven_parts(rng, count, total, limit, skew):
    if count == 2:
        one = jax.random.randint(rng, (), max(1, total - limit), min(limit, total - 1) + 1)
        return jnp.stack([one, total - one])
    sizes = jnp.asarray(profile(count, total, limit, skew), jnp.int32)
    pairs = (count - 1) // 2
    source_of, sink = sizes[1:1 + 2 * pairs:2], sizes[2:2 + 2 * pairs:2]
    margin = jnp.minimum(source_of - 1, limit - sink)
    moved = jax.random.randint(jax.random.fold_in(rng, 1), (pairs,), 0, 1 << 20) % (margin + 1)
    sizes = sizes.at[1:1 + 2 * pairs:2].set(source_of - moved).at[2:2 + 2 * pairs:2].set(sink + moved)
    return sizes[jax.random.permutation(jax.random.fold_in(rng, 2), count)]


def noise(own_key, extent, deviation, bound, cuts=(), held_as=jnp.bfloat16):
    level = block_levels(own_key, extent, cuts, -0.22, 0.18) if cuts else 1.0
    drawn = jax.random.normal(own_key, extent, jnp.float32) * deviation * level
    return jnp.minimum(jnp.maximum(drawn, -bound), bound).astype(held_as)


def heavy_noise(own_key, extent, width, reach, cuts, heavy, kind=jnp.bfloat16):
    drawn = width * jax.random.normal(own_key, extent, jnp.float32)
    if cuts:
        drawn = drawn * block_levels(own_key, extent, cuts, -0.22, 0.18)
    return jnp.clip(spiked(drawn, jax.random.fold_in(own_key, 3), *heavy), -reach, reach).astype(kind)


def setup_inputs(seed: int = 0) -> dict:
    keys = jax.random.split(jax.random.key(seed), 17)
    return {
        "block_input": noise(keys[0], (SEQS, SEQ_LEN, D), 1.0, 6.0, ((0, 8), (1, 4))),
        "segment_ids": jax.vmap(lambda own: jnp.searchsorted(jnp.cumsum(uneven_parts(own, 3, SEQ_LEN, SEQ_LEN // 2 + SEQ_LEN // 8, 0)), jnp.arange(SEQ_LEN), side="right"))(jax.random.split(keys[1], SEQS)).reshape((SEQS, SEQ_LEN)).astype(jnp.int32),
        "ln1_gain": jnp.clip(1.0 + 0.15 * jax.random.normal(keys[2], (D,), jnp.float32), 0.25, 1.75).astype(jnp.bfloat16),
        "ln1_bias": noise(keys[3], (D,), 0.5, 3.0, ((0, 8),)),
        "qkv_weight": draw_qkv_weight(jax.random.fold_in(keys[16], 71), 0),
        "query_bias": noise(keys[5], (D,), 0.5, 3.0, ((0, 8),)),
        "value_bias": noise(keys[6], (D,), 0.2, 1.1953125, ((0, 8),)),
        "proj_weight": noise(keys[7], (D, D), (max(D // 16, 4)) ** -0.5, 0.75, ((0, 4), (1, 8))),
        "proj_bias": noise(keys[8], (D,), 0.5, 3.0, ((0, 8),)),
        "ln2_gain": jnp.clip(1.0 + 0.15 * jax.random.normal(keys[9], (D,), jnp.float32), 0.25, 1.75).astype(jnp.bfloat16),
        "ln2_bias": noise(keys[10], (D,), 0.5, 3.0, ((0, 8),)),
        "fc_weight": noise(keys[11], (D, FF), D ** -0.5, 0.1875, ((0, 8), (1, 4))),
        "fc_bias": noise(keys[12], (FF,), 0.5, 3.0, ((0, 8),)),
        "out_weight": noise(keys[13], (FF, D), FF ** -0.5, 0.09375, ((0, 4), (1, 8))),
        "out_bias": noise(keys[14], (D,), 0.5, 3.0, ((0, 8),)),
        "cotangent": heavy_noise(keys[15], (SEQS, SEQ_LEN, D), 1.0, 6.0, ((0, 8), (1, 4)), (0, 2, 8, 2.0)),
    }


NORM_EPS = 1e-05
GELU_ROOT = math.sqrt(2.0 / math.pi)
GELU_CUBE = 0.044715
MASK_VALUE = -1e+30

def norm_forward(residual):
    row_mean = lax.optimization_barrier(jnp.mean(residual, axis=-1, keepdims=True))
    centered = residual - row_mean
    row_var = lax.optimization_barrier(jnp.mean(centered * centered, axis=-1, keepdims=True))
    inv_std = lax.rsqrt(row_var + NORM_EPS)
    return (centered * inv_std, inv_std)

def norm_backward(grad_in, normed, inv_std, gain):
    scaled = grad_in * gain
    mean_scaled = lax.optimization_barrier(jnp.mean(scaled, axis=-1, keepdims=True))
    mean_cross = lax.optimization_barrier(jnp.mean(scaled * normed, axis=-1, keepdims=True))
    return inv_std * (scaled - mean_scaled - normed * mean_cross)

def gelu_pair(pre_act):
    inner_arg = GELU_ROOT * (pre_act + GELU_CUBE * pre_act * pre_act * pre_act)
    tangent = jnp.tanh(inner_arg)
    activated = 0.5 * pre_act * (1.0 + tangent)
    gelu_slope = 0.5 * (1.0 + tangent) + 0.5 * pre_act * (1.0 - tangent * tangent) * GELU_ROOT * (1.0 + 3.0 * GELU_CUBE * pre_act * pre_act)
    return (activated, gelu_slope)

def reference(block_input, segment_ids, ln1_gain, ln1_bias, qkv_weight, query_bias, value_bias, proj_weight, proj_bias, ln2_gain, ln2_bias, fc_weight, fc_bias, out_weight, out_bias, cotangent):
    qkv_flat = qkv_weight.reshape(D, 3 * D)
    gain_first = ln1_gain.astype(jnp.float32)
    shift_first = ln1_bias.astype(jnp.float32)
    query_shift = query_bias.astype(jnp.float32)
    value_shift = value_bias.astype(jnp.float32)
    proj_shift = proj_bias.astype(jnp.float32)
    gain_second = ln2_gain.astype(jnp.float32)
    shift_second = ln2_bias.astype(jnp.float32)
    fc_shift = fc_bias.astype(jnp.float32)
    out_shift = out_bias.astype(jnp.float32)
    positions = jnp.arange(SEQ_LEN, dtype=jnp.int32)
    score_scale = HD ** (-0.5)

    def one_sequence(totals, inputs):
        tokens, seg_row, grad_rows = inputs
        allowed = (positions[:, None] >= positions[None, :]) & (seg_row[:, None] == seg_row[None, :])
        resid_in = tokens.astype(jnp.float32)
        normed_one, inv_one = norm_forward(resid_in)
        hidden_one = (normed_one * gain_first + shift_first).astype(jnp.bfloat16)
        qkv_out = jnp.dot(hidden_one, qkv_flat, preferred_element_type=jnp.float32)
        queries = (qkv_out[:, :D] + query_shift).astype(jnp.bfloat16)
        keys_all = qkv_out[:, D:2 * D].astype(jnp.bfloat16)
        values_all = (qkv_out[:, 2 * D:] + value_shift).astype(jnp.bfloat16)
        query_heads = queries.astype(jnp.float32).reshape(SEQ_LEN, HEADS, HD)
        key_heads = keys_all.astype(jnp.float32).reshape(SEQ_LEN, HEADS, HD)
        value_heads = values_all.astype(jnp.float32).reshape(SEQ_LEN, HEADS, HD)
        raw_scores = jnp.einsum('qhd,khd->hqk', query_heads, key_heads) * score_scale
        scores = jnp.where(allowed[None], raw_scores, MASK_VALUE)
        top_score = lax.optimization_barrier(jnp.max(scores, axis=-1, keepdims=True))
        log_total = top_score + jnp.log(lax.optimization_barrier(jnp.sum(jnp.exp(scores - top_score), axis=-1, keepdims=True)))
        attn_probs = jnp.where(allowed[None], jnp.exp(scores - log_total), 0.0)
        probs_half = attn_probs.astype(jnp.bfloat16)
        attended = jnp.einsum('hqk,khd->qhd', probs_half.astype(jnp.float32), value_heads).reshape(SEQ_LEN, D).astype(jnp.bfloat16)
        resid_mid = resid_in + jnp.dot(attended, proj_weight, preferred_element_type=jnp.float32) + proj_shift
        normed_two, inv_two = norm_forward(resid_mid)
        hidden_two = (normed_two * gain_second + shift_second).astype(jnp.bfloat16)
        pre_act = jnp.dot(hidden_two, fc_weight, preferred_element_type=jnp.float32) + fc_shift
        activated, gelu_slope = gelu_pair(pre_act)
        activated = activated.astype(jnp.bfloat16)
        block_output = (resid_mid + jnp.dot(activated, out_weight, preferred_element_type=jnp.float32) + out_shift).astype(jnp.bfloat16)
        grad_out = grad_rows.astype(jnp.float32)
        out_shift_grad = lax.optimization_barrier(jnp.sum(grad_out, axis=0))
        out_weight_grad = jnp.dot(activated.T, grad_rows, preferred_element_type=jnp.float32)
        pre_grad = jnp.dot(grad_rows, out_weight.T, preferred_element_type=jnp.float32) * gelu_slope
        fc_shift_grad = lax.optimization_barrier(jnp.sum(pre_grad, axis=0))
        pre_grad_half = pre_grad.astype(jnp.bfloat16)
        fc_weight_grad = jnp.dot(hidden_two.T, pre_grad_half, preferred_element_type=jnp.float32)
        hidden_two_grad = jnp.dot(pre_grad_half, fc_weight.T, preferred_element_type=jnp.float32)
        gain_second_grad = lax.optimization_barrier(jnp.sum(hidden_two_grad * normed_two, axis=0))
        shift_second_grad = lax.optimization_barrier(jnp.sum(hidden_two_grad, axis=0))
        mid_grad = grad_out + norm_backward(hidden_two_grad, normed_two, inv_two, gain_second)
        proj_shift_grad = lax.optimization_barrier(jnp.sum(mid_grad, axis=0))
        mid_grad_half = mid_grad.astype(jnp.bfloat16)
        proj_weight_grad = jnp.dot(attended.T, mid_grad_half, preferred_element_type=jnp.float32)
        attended_grad = jnp.dot(mid_grad_half, proj_weight.T, preferred_element_type=jnp.float32).astype(jnp.bfloat16)
        grad_heads = attended_grad.astype(jnp.float32).reshape(SEQ_LEN, HEADS, HD)
        prob_grad = jnp.einsum('qhd,khd->hqk', grad_heads, value_heads)
        value_grad = jnp.einsum('hqk,qhd->khd', probs_half.astype(jnp.float32), grad_heads).reshape(SEQ_LEN, D)
        delta_rows = lax.optimization_barrier(jnp.sum(attn_probs * prob_grad, axis=-1, keepdims=True))
        score_grad = (attn_probs * (prob_grad - delta_rows) * score_scale).astype(jnp.bfloat16).astype(jnp.float32)
        query_grad = jnp.einsum('hqk,khd->qhd', score_grad, key_heads).reshape(SEQ_LEN, D)
        key_grad = jnp.einsum('hqk,qhd->khd', score_grad, query_heads).reshape(SEQ_LEN, D)
        query_shift_grad = lax.optimization_barrier(jnp.sum(query_grad, axis=0))
        value_shift_grad = lax.optimization_barrier(jnp.sum(value_grad, axis=0))
        qkv_grad = jnp.concatenate([query_grad, key_grad, value_grad], axis=1).astype(jnp.bfloat16)
        qkv_weight_grad = jnp.dot(hidden_one.T, qkv_grad, preferred_element_type=jnp.float32)
        hidden_one_grad = jnp.dot(qkv_grad, qkv_flat.T, preferred_element_type=jnp.float32)
        gain_first_grad = lax.optimization_barrier(jnp.sum(hidden_one_grad * normed_one, axis=0))
        shift_first_grad = lax.optimization_barrier(jnp.sum(hidden_one_grad, axis=0))
        input_grad = mid_grad + norm_backward(hidden_one_grad, normed_one, inv_one, gain_first)
        terms = (gain_first_grad, shift_first_grad, qkv_weight_grad, query_shift_grad, value_shift_grad, proj_weight_grad, proj_shift_grad, gain_second_grad, shift_second_grad, fc_weight_grad, fc_shift_grad, out_weight_grad, out_shift_grad)
        new_totals = tuple((total + term for total, term in zip(totals, terms)))
        return (new_totals, (block_output, input_grad))
    zero_init = (jnp.zeros((D,), jnp.float32), jnp.zeros((D,), jnp.float32), jnp.zeros((D, 3 * D), jnp.float32), jnp.zeros((D,), jnp.float32), jnp.zeros((D,), jnp.float32), jnp.zeros((D, D), jnp.float32), jnp.zeros((D,), jnp.float32), jnp.zeros((D,), jnp.float32), jnp.zeros((D,), jnp.float32), jnp.zeros((D, FF), jnp.float32), jnp.zeros((FF,), jnp.float32), jnp.zeros((FF, D), jnp.float32), jnp.zeros((D,), jnp.float32))
    totals, outputs = lax.scan(one_sequence, zero_init, (block_input, segment_ids, cotangent))
    block_output, input_grad = outputs
    return (block_output, input_grad, totals[0], totals[1], totals[2].reshape(D, 3, D), totals[3], totals[4], totals[5], totals[6], totals[7], totals[8], totals[9], totals[10], totals[11], totals[12])
```

```python
import functools
import jax
import jax.numpy as jnp
from jax import lax
from jax.experimental import pallas as pl
from jax.experimental.pallas import tpu as pltpu
from jax.sharding import PartitionSpec as P

D = 1024
HD = 64
FF = 4096


NORM_EPS = 1e-05
GELU_ROOT = 0.7978845608028654
GELU_CUBE = 0.044715
MASK_VALUE = -1e30


def norm_forward(residual):
    row_mean = jnp.mean(residual, axis=-1, keepdims=True)
    centered = residual - row_mean
    row_var = jnp.mean(centered * centered, axis=-1, keepdims=True)
    inv_std = lax.rsqrt(row_var + NORM_EPS)
    return (centered * inv_std, inv_std)


def norm_backward(grad_in, normed, inv_std, gain):
    scaled = grad_in * gain
    mean_scaled = jnp.mean(scaled, axis=-1, keepdims=True)
    mean_cross = jnp.mean(scaled * normed, axis=-1, keepdims=True)
    return inv_std * (scaled - mean_scaled - normed * mean_cross)


def gelu_pair(pre_act):
    inner_arg = GELU_ROOT * (pre_act + GELU_CUBE * pre_act * pre_act * pre_act)
    tangent = jnp.tanh(inner_arg)
    activated = 0.5 * pre_act * (1.0 + tangent)
    gelu_slope = 0.5 * (1.0 + tangent) + 0.5 * pre_act * (1.0 - tangent * tangent) * GELU_ROOT * (
        1.0 + 3.0 * GELU_CUBE * pre_act * pre_act
    )
    return (activated, gelu_slope)


def masked_scores(query_heads, key_heads, allowed):
    raw_scores = jnp.einsum(
        "qhd,khd->hqk", query_heads, key_heads, preferred_element_type=jnp.float32
    ) * HD ** (-0.5)
    return jnp.where(allowed[None], raw_scores, MASK_VALUE)


def attend(query_heads, key_heads, value_heads, allowed):
    scores = masked_scores(query_heads, key_heads, allowed)
    top_score = jnp.max(scores, axis=-1, keepdims=True)
    log_total = top_score + jnp.log(jnp.sum(jnp.exp(scores - top_score), axis=-1, keepdims=True))
    attn_probs = jnp.where(allowed[None], jnp.exp(scores - log_total), 0.0)
    probs_half = attn_probs.astype(jnp.bfloat16)
    attended = jnp.einsum(
        "hqk,khd->qhd", probs_half, value_heads, preferred_element_type=jnp.float32
    )
    return (attended.reshape(query_heads.shape[0], -1).astype(jnp.bfloat16), log_total)


def attend_back(query_heads, key_heads, value_heads, allowed, log_total, grad_heads):
    scores = masked_scores(query_heads, key_heads, allowed)
    attn_probs = jnp.where(allowed[None], jnp.exp(scores - log_total), 0.0)
    probs_half = attn_probs.astype(jnp.bfloat16)
    prob_grad = jnp.einsum(
        "qhd,khd->hqk", grad_heads, value_heads, preferred_element_type=jnp.float32
    )
    value_part = jnp.einsum(
        "hqk,qhd->khd", probs_half, grad_heads, preferred_element_type=jnp.float32
    )
    delta_rows = jnp.sum(attn_probs * prob_grad, axis=-1, keepdims=True)
    score_grad = (attn_probs * (prob_grad - delta_rows) * HD ** (-0.5)).astype(jnp.bfloat16)
    query_grad = jnp.einsum(
        "hqk,khd->qhd", score_grad, key_heads, preferred_element_type=jnp.float32
    )
    key_part = jnp.einsum(
        "hqk,qhd->khd", score_grad, query_heads, preferred_element_type=jnp.float32
    )
    key_count = key_heads.shape[0]
    return (
        query_grad.reshape(query_heads.shape[0], -1),
        key_part.reshape(key_count, -1),
        value_part.reshape(key_count, -1),
    )


def place_part(part, whole_len, start):
    return lax.dynamic_update_slice_in_dim(jnp.zeros((whole_len,), jnp.float32), part, start, 0)


def body(
    block_input,
    segment_ids,
    ln1_gain,
    ln1_bias,
    qkv_weight,
    query_bias,
    value_bias,
    proj_weight,
    proj_bias,
    ln2_gain,
    ln2_bias,
    fc_weight,
    fc_bias,
    out_weight,
    out_bias,
    cotangent,
):
    tokens = block_input[0]
    seg_whole = segment_ids[0]
    grad_rows = cotangent[0]
    seq_length = seg_whole.shape[0]
    ctx_rank = lax.axis_index("ctx")
    key_pos = jnp.arange(seq_length, dtype=jnp.int32)
    resid_in = tokens.astype(jnp.float32)
    normed_one, inv_one = norm_forward(resid_in)
    grad_out = grad_rows.astype(jnp.float32)
    out_shift_grad = jnp.sum(grad_out, axis=0)
    vectors = lax.all_gather(
        jnp.concatenate(
            [ln1_gain, ln1_bias, query_bias, value_bias, proj_bias, ln2_gain, ln2_bias, out_bias, fc_bias]
        ),
        "dp",
        axis=0,
    )
    slice_len = ln1_gain.shape[0]
    dp_size = vectors.shape[0]
    ff_whole = fc_bias.shape[0] * dp_size

    def vector(at):
        return vectors[:, at * slice_len : (at + 1) * slice_len].astype(jnp.float32).reshape(-1)

    qkv_cols = lax.all_gather(qkv_weight, "dp", axis=0, tiled=True).reshape(D, -1)
    proj_rows = lax.all_gather(proj_weight, "dp", axis=1, tiled=True)
    fc_cols = lax.all_gather(fc_weight, "dp", axis=0, tiled=True)
    out_rows = lax.all_gather(out_weight, "dp", axis=1, tiled=True)
    quarter = proj_rows.shape[0]
    unit_part = fc_cols.shape[1]
    gain_first = vector(0)
    shift_first = vector(1)
    query_shift = lax.dynamic_slice_in_dim(vector(2), ctx_rank * quarter, quarter)
    value_shift = lax.dynamic_slice_in_dim(vector(3), ctx_rank * quarter, quarter)
    proj_shift = vector(4)
    gain_second = vector(5)
    shift_second = vector(6)
    out_shift = vector(7)
    fc_shift = lax.dynamic_slice_in_dim(
        vectors[:, 8 * slice_len :].astype(jnp.float32).reshape(-1), ctx_rank * unit_part, unit_part
    )
    local_heads = quarter // HD
    allowed = (key_pos[:, None] >= key_pos[None, :]) & (seg_whole[:, None] == seg_whole[None, :])
    hidden_one = (normed_one * gain_first + shift_first).astype(jnp.bfloat16)
    hidden_all, grad_all = (
        lax.all_gather(hidden_one, "ctx", axis=0, tiled=True),
        lax.all_gather(grad_rows, "ctx", axis=0, tiled=True),
    )
    qkv_out = jnp.dot(hidden_all, qkv_cols, preferred_element_type=jnp.float32)
    queries = (qkv_out[:, :quarter] + query_shift).astype(jnp.bfloat16)
    keys_here = qkv_out[:, quarter : 2 * quarter].astype(jnp.bfloat16)
    values_here = (qkv_out[:, 2 * quarter :] + value_shift).astype(jnp.bfloat16)
    query_heads = queries.reshape(seq_length, local_heads, HD)
    key_heads = keys_here.reshape(seq_length, local_heads, HD)
    value_heads = values_here.reshape(seq_length, local_heads, HD)
    attended, log_total = attend(query_heads, key_heads, value_heads, allowed)
    resid_mid = (
        resid_in
        + lax.psum_scatter(
            jnp.dot(attended, proj_rows, preferred_element_type=jnp.float32).astype(jnp.bfloat16),
            "ctx",
            scatter_dimension=0,
            tiled=True,
        ).astype(jnp.float32)
        + proj_shift
    )
    normed_two, inv_two = norm_forward(resid_mid)
    hidden_two = (normed_two * gain_second + shift_second).astype(jnp.bfloat16)
    hidden_two_all = lax.all_gather(hidden_two, "ctx", axis=0, tiled=True)
    pre_act = jnp.dot(hidden_two_all, fc_cols, preferred_element_type=jnp.float32) + fc_shift
    activated, gelu_slope = gelu_pair(pre_act)
    activated = activated.astype(jnp.bfloat16)
    block_output = (
        resid_mid
        + lax.psum_scatter(
            jnp.dot(activated, out_rows, preferred_element_type=jnp.float32).astype(jnp.bfloat16),
            "ctx",
            scatter_dimension=0,
            tiled=True,
        ).astype(jnp.float32)
        + out_shift
    ).astype(jnp.bfloat16)
    out_weight_grad = jnp.dot(activated.T, grad_all, preferred_element_type=jnp.float32)
    pre_grad = jnp.dot(grad_all, out_rows.T, preferred_element_type=jnp.float32) * gelu_slope
    fc_shift_grad = place_part(jnp.sum(pre_grad, axis=0), ff_whole, ctx_rank * unit_part)
    pre_grad_half = pre_grad.astype(jnp.bfloat16)
    fc_weight_grad = jnp.dot(hidden_two_all.T, pre_grad_half, preferred_element_type=jnp.float32)
    hidden_two_grad = lax.psum_scatter(
        jnp.dot(pre_grad_half, fc_cols.T, preferred_element_type=jnp.float32).astype(jnp.bfloat16),
        "ctx",
        scatter_dimension=0,
        tiled=True,
    ).astype(jnp.float32)
    gain_second_grad = jnp.sum(hidden_two_grad * normed_two, axis=0)
    shift_second_grad = jnp.sum(hidden_two_grad, axis=0)
    mid_grad = grad_out + norm_backward(hidden_two_grad, normed_two, inv_two, gain_second)
    proj_shift_grad = jnp.sum(mid_grad, axis=0)
    mid_grad_half = mid_grad.astype(jnp.bfloat16)
    mid_all = lax.all_gather(mid_grad_half, "ctx", axis=0, tiled=True)
    proj_weight_grad = jnp.dot(attended.T, mid_all, preferred_element_type=jnp.float32)
    attended_grad = jnp.dot(mid_all, proj_rows.T, preferred_element_type=jnp.float32).astype(
        jnp.bfloat16
    )
    grad_heads = attended_grad.reshape(seq_length, local_heads, HD)
    query_grad, key_grad, value_grad = attend_back(
        query_heads, key_heads, value_heads, allowed, log_total, grad_heads
    )
    query_shift_grad = place_part(jnp.sum(query_grad, axis=0), D, ctx_rank * quarter)
    value_shift_grad = place_part(jnp.sum(value_grad, axis=0), D, ctx_rank * quarter)
    qkv_grad = jnp.concatenate([query_grad, key_grad, value_grad], axis=1).astype(jnp.bfloat16)
    qkv_weight_grad = jnp.dot(hidden_all.T, qkv_grad, preferred_element_type=jnp.float32).reshape(
        D, 3, quarter
    )
    hidden_one_grad = lax.psum_scatter(
        jnp.dot(qkv_grad, qkv_cols.T, preferred_element_type=jnp.float32).astype(jnp.bfloat16),
        "ctx",
        scatter_dimension=0,
        tiled=True,
    ).astype(jnp.float32)
    gain_first_grad = jnp.sum(hidden_one_grad * normed_one, axis=0)
    shift_first_grad = jnp.sum(hidden_one_grad, axis=0)
    input_grad = mid_grad + norm_backward(hidden_one_grad, normed_one, inv_one, gain_first)
    half = jnp.bfloat16
    matrix_sums = (
        lax.psum_scatter(qkv_weight_grad.astype(half), "dp", scatter_dimension=0, tiled=True),
        lax.psum_scatter(proj_weight_grad.astype(half), "dp", scatter_dimension=1, tiled=True),
        lax.psum_scatter(fc_weight_grad.astype(half), "dp", scatter_dimension=0, tiled=True),
        lax.psum_scatter(out_weight_grad.astype(half), "dp", scatter_dimension=1, tiled=True),
    )
    matrix_sums = tuple(m.astype(jnp.float32) for m in matrix_sums)
    packed = jnp.concatenate(
        [
            v.reshape(dp_size, -1)
            for v in (
                gain_first_grad,
                shift_first_grad,
                query_shift_grad,
                value_shift_grad,
                proj_shift_grad,
                gain_second_grad,
                shift_second_grad,
                out_shift_grad,
                fc_shift_grad,
            )
        ],
        axis=1,
    )
    packed = lax.psum(packed, ("dp", "ctx"))
    mine = lax.dynamic_index_in_dim(packed, lax.axis_index("dp"), 0, keepdims=False)
    order = (0, 1, 2, 3, 4, 5, 6, 8, 7)
    pieces = [mine[i * slice_len : (i + 1) * slice_len] for i in range(8)] + [mine[8 * slice_len :]]
    vector_sums = tuple(pieces[i] for i in order)
    return (
        block_output[None],
        input_grad[None],
        vector_sums[0],
        vector_sums[1],
        matrix_sums[0],
        vector_sums[2],
        vector_sums[3],
        matrix_sums[1],
        vector_sums[4],
        vector_sums[5],
        vector_sums[6],
        matrix_sums[2],
        vector_sums[7],
        matrix_sums[3],
        vector_sums[8],
    )


NX = 2
NZ = 4
NDP = NX * NZ
NC = 4
T = 128
S = NC * T
W = 128
Q = D // NC
U = FF // NC
HEADS_HERE = Q // HD
BLK = 256
MESH = pl.DeviceIdType.MESH
F32 = jnp.float32
BF16 = jnp.bfloat16
VEC_ROWS = 16


def fits(mesh):
    return mesh.shape["dp"] == NDP and mesh.shape["ctx"] == NC


def dot(a, b):
    return jnp.dot(a, b, preferred_element_type=F32)


def dot_nt(a, b):
    return lax.dot_general(a, b, (((1,), (1,)), ((), ())), preferred_element_type=F32)


def dot_tn(a, b):
    return lax.dot_general(a, b, (((0,), (0,)), ((), ())), preferred_element_type=F32)


def fused_kernel(
    x_ref, cot_ref, seg_row_ref, seg_col_ref, vec_ref, qkv_ref, proj_ref, fc_ref, outw_ref,
    block_out, input_grad_out, g_qkv, g_proj, g_fc, g_out, vec_out,
    vec_g, qkv_g, proj_g, fc_g, out_g,
    h_all, cot_all, h2_all, mid_all, xt_h, xt_cot, xt_h2, xt_mid,
    q_s, k_s, v_s, att_s, p_s, bias_s, act_s, slope_s, pgh_s, ag_s, dqkv_s,
    resid_s, normed1_s, inv1_s, normed2_s, inv2_s, midg_s,
    rs_a, rs_b, rs_c, rs_d, rr_a, rr_b, rr_c, rr_d,
    xs_qkv, xs_proj, xs_fc, xs_out, xr_qkv, xr_proj, xr_fc, xr_out,
    zs_qkv, zs_proj, zs_fc, zs_out, zr_qkv, zr_proj, zr_fc, zr_out,
    vp, vxr, vzs, vzr, vcs, vcr,
    ssem, rsem,
):
    dp = lax.axis_index("dp")
    c = lax.axis_index("ctx")
    z = dp // NX
    x = dp % NX
    xo = 1 - x

    def zat(r):
        return (z + r) % NZ

    def chunk(zz, xx):
        return zz * NX + xx

    def span(i, n):
        return pl.ds(pl.multiple_of(i * n, n), n)

    counter = [0]
    sends = []

    def sem_block(n):
        base = counter[0]
        counter[0] += n
        return base

    def remote(src, dst, sem, dev):
        return pltpu.make_async_remote_copy(
            src_ref=src, dst_ref=dst, send_sem=ssem.at[sem], recv_sem=rsem.at[sem],
            device_id=dev, device_id_type=MESH,
        )

    def send(src, dst, sem, dev):
        copy = remote(src, dst, sem, dev)
        copy.start()
        sends.append(copy)

    x_dev = (chunk(z, xo), c)

    def z_dev(r):
        return (chunk(zat(r), x), c)

    def c_dev(r):
        return (dp, (c + r) % NC)

    def wait_recv(dst, sem):
        remote(dst, dst, sem, x_dev).wait_recv()

    class Gather:
        def __init__(self, shard, slot):
            self.shard, self.slot, self.base = shard, slot, sem_block(7)

        def start_z(self):
            for r in (1, 3, 2):
                send(self.shard, self.slot(dp), self.base + r - 1, z_dev(r))

        def start_x(self):
            send(self.shard, self.slot(dp), self.base + 3, x_dev)

        def forward(self, r):
            here = self.slot(chunk(zat(NZ - r), x))
            wait_recv(here, self.base + r - 1)
            send(here, here, self.base + 3 + r, x_dev)

        def finish(self):
            wait_recv(self.slot(chunk(z, xo)), self.base + 3)
            for r in (1, 3, 2):
                wait_recv(self.slot(chunk(zat(NZ - r), xo)), self.base + 3 + r)

    def rows_slot(buf):
        return lambda d: buf.at[span(d, W)]

    def cols_slot(buf):
        return lambda d: buf.at[:, span(d, W)]

    vec_ag = Gather(vec_ref, lambda d: vec_g.at[d])
    qkv_ag = Gather(qkv_ref, rows_slot(qkv_g))
    proj_ag = Gather(proj_ref, cols_slot(proj_g))
    fc_ag = Gather(fc_ref, rows_slot(fc_g))
    out_ag = Gather(outw_ref, cols_slot(out_g))

    class Reduce:
        def __init__(self, left, right, xs, xr, zs, zr, width):
            self.left, self.right, self.width = left, right, width
            self.xs, self.xr, self.zs, self.zr = xs, xr, zs, zr
            self.xbase, self.zbase = sem_block(NZ), sem_block(NZ - 1)

        def part(self, d):
            return dot(self.left[span(d, W), :], self.right[...])

        def to_x(self):
            for j in range(NZ):
                self.xs[j] = self.part(chunk(j, xo)).astype(BF16)
                send(self.xs.at[j], self.xr.at[j], self.xbase + j, x_dev)

        def to_z(self):
            for j in range(NZ):
                wait_recv(self.xr.at[j], self.xbase + j)
            for r in (2, 1, 3):
                zz = zat(r)
                total = self.part(chunk(zz, x)) + self.xr[zz].astype(F32)
                self.zs[r] = total.astype(BF16)
                send(self.zs.at[r], self.zr.at[r], self.zbase + r - 1, z_dev(r))

        def total(self):
            own = self.part(chunk(z, x)) + self.xr[z].astype(F32)
            for r in (1, 3, 2):
                wait_recv(self.zr.at[r], self.zbase + r - 1)
                own = own + self.zr[r].astype(F32)
            return own

    out_rs = Reduce(xt_cot, act_s, xs_out, xr_out, zs_out, zr_out, U)
    fc_rs = Reduce(xt_h2, pgh_s, xs_fc, xr_fc, zs_fc, zr_fc, U)
    proj_rs = Reduce(xt_mid, att_s, xs_proj, xr_proj, zs_proj, zr_proj, Q)
    qkv_rs = Reduce(xt_h, dqkv_s, xs_qkv, xr_qkv, zs_qkv, zr_qkv, 3 * Q)
    vec_xbase, vec_zbase, vec_cbase = sem_block(NZ), sem_block(NZ), sem_block(NC)

    class Share:
        def __init__(self, buf):
            self.buf, self.base = buf, sem_block(NC - 1)

        def start(self):
            here = self.buf.at[span(c, T)]
            for r in (2, 1, 3):
                send(here, here, self.base + r - 1, c_dev(r))

        def finish(self):
            for r in (1, 2, 3):
                wait_recv(self.buf.at[span((c + NC - r) % NC, T)], self.base + r - 1)

    class Scatter:
        def __init__(self, full, got):
            self.full, self.got, self.base = full, got, sem_block(NC - 1)

        def start(self):
            for r in (2, 1, 3):
                send(self.full.at[span((c + r) % NC, T)], self.got.at[r], self.base + r - 1, c_dev(r))

        def finish(self):
            total = self.full[span(c, T), :].astype(F32)
            for r in (1, 2, 3):
                wait_recv(self.got.at[r], self.base + r - 1)
                total = total + self.got[r].astype(F32)
            return total

    h_share, cot_share, h2_share, mid_share = Share(h_all), Share(cot_all), Share(h2_all), Share(mid_all)
    proj_sc, out_sc, h2g_sc, h1g_sc = (
        Scatter(rs_a, rr_a), Scatter(rs_b, rr_b), Scatter(rs_c, rr_c), Scatter(rs_d, rr_d)
    )

    barrier = pltpu.get_barrier_semaphore()
    peers = [z_dev(r) for r in (1, 2, 3)] + [x_dev] + [c_dev(r) for r in (1, 2, 3)]
    for dev in peers:
        pl.semaphore_signal(barrier, inc=1, device_id=dev, device_id_type=MESH)
    pl.semaphore_wait(barrier, len(peers))

    vec_ag.start_z()
    vec_ag.start_x()
    vec_g[dp] = vec_ref[...]
    qkv_ag.start_z()
    qkv_ag.start_x()
    proj_ag.start_z()
    fc_ag.start_z()
    out_ag.start_z()

    qkv_g[span(dp, W), :] = qkv_ref[...]
    proj_g[:, span(dp, W)] = proj_ref[...]
    fc_g[span(dp, W), :] = fc_ref[...]
    out_g[:, span(dp, W)] = outw_ref[...]
    resid_in = x_ref[...].astype(F32)
    normed, inv = norm_forward(resid_in)
    normed1_s[...] = normed
    inv1_s[...] = inv
    cot_all[span(c, T), :] = cot_ref[...]
    key_pos = lax.broadcasted_iota(jnp.int32, (S, S), 1)
    query_pos = lax.broadcasted_iota(jnp.int32, (S, S), 0)
    allowed = (query_pos >= key_pos) & (seg_col_ref[...] == seg_row_ref[...])
    bias_s[...] = jnp.where(allowed, 0.0, MASK_VALUE)
    vp[...] = jnp.zeros_like(vp)

    for r in (1, 3, 2):
        vec_ag.forward(r)
    vec_ag.finish()
    vectors = vec_g[...].astype(F32)

    def vector(row):
        return jnp.concatenate([vectors[d, row : row + 1, :] for d in range(NDP)], axis=1)

    gain1, shift1 = vector(0), vector(1)
    h_all[span(c, T), :] = (normed * gain1 + shift1).astype(BF16)
    h_share.start()
    cot_share.start()

    for r in (1, 3, 2):
        qkv_ag.forward(r)
    proj_ag.start_x()
    fc_ag.start_x()
    h_share.finish()
    qkv_ag.finish()

    def quarter_vector(row):
        first = vec_g[2 * c].astype(F32)[row : row + 1, :]
        second = vec_g[2 * c + 1].astype(F32)[row : row + 1, :]
        return jnp.concatenate([first, second], axis=1)

    q_s[...] = ((dot(h_all[...], qkv_g[:, :Q]) + quarter_vector(2)).astype(BF16).astype(F32) * HD ** (-0.5)).astype(BF16)
    k_s[...] = dot(h_all[...], qkv_g[:, Q : 2 * Q]).astype(BF16)
    v_s[...] = (dot(h_all[...], qkv_g[:, 2 * Q :]) + quarter_vector(3)).astype(BF16)

    for r in (1, 3, 2):
        proj_ag.forward(r)

    for h in range(HEADS_HERE):
        cols = slice(h * HD, (h + 1) * HD)
        for b in range(S // BLK):
            rows, upto = slice(b * BLK, (b + 1) * BLK), (b + 1) * BLK
            scores = dot_nt(q_s[rows, cols], k_s[:upto, cols]) + bias_s[rows, :upto]
            top = jnp.max(scores, axis=-1, keepdims=True)
            weights = jnp.exp(scores - top)
            probs = weights * (1.0 / jnp.sum(weights, axis=-1, keepdims=True))
            p_s[h, rows, :upto] = probs
            att_s[rows, cols] = dot(probs.astype(BF16), v_s[:upto, cols]).astype(BF16)

    proj_ag.finish()
    for i in range(D // 256):
        cols = slice(i * 256, (i + 1) * 256)
        rs_a[:, cols] = dot(att_s[...], proj_g[:, cols]).astype(BF16)
    proj_sc.start()
    xt_h[...] = h_all[...].T
    cot_share.finish()
    xt_cot[...] = cot_all[...].T
    for r in (1, 3, 2):
        fc_ag.forward(r)
    out_ag.start_x()

    resid_mid = x_ref[...].astype(F32) + proj_sc.finish() + vector(4)
    resid_s[...] = resid_mid
    normed, inv = norm_forward(resid_mid)
    normed2_s[...] = normed
    inv2_s[...] = inv
    h2_all[span(c, T), :] = (normed * vector(5) + vector(6)).astype(BF16)
    h2_share.start()
    fc_ag.finish()
    h2_share.finish()

    def fc_vector():
        pieces = []
        for i in range(2):
            block = vec_g[2 * c + i].astype(F32)
            pieces += [block[8 + k : 9 + k, :] for k in range(4)]
        return jnp.concatenate(pieces, axis=1)

    fc_shift = fc_vector()
    for i in range(U // 256):
        cols = slice(i * 256, (i + 1) * 256)
        activated, slope = gelu_pair(dot(h2_all[...], fc_g[:, cols]) + fc_shift[:, cols])
        act_s[:, cols] = activated.astype(BF16)
        slope_s[:, cols] = slope
    xt_h2[...] = h2_all[...].T

    for r in (1, 3, 2):
        out_ag.forward(r)
    out_rs.to_x()
    out_ag.finish()

    def put_quarter(row, total):
        for i in range(2):
            vp[2 * c + i, row : row + 1, :] = total[:, i * W : (i + 1) * W]

    def put_whole(row, total):
        for d in range(NDP):
            vp[d, row : row + 1, :] = total[:, d * W : (d + 1) * W]

    sums = []
    for i in range(U // 256):
        cols = slice(i * 256, (i + 1) * 256)
        pre_grad = dot_nt(cot_all[...], out_g[cols, :]) * slope_s[:, cols]
        sums.append(jnp.sum(pre_grad, axis=0, keepdims=True))
        pgh_s[:, cols] = pre_grad.astype(BF16)
    fc_sum = jnp.concatenate(sums, axis=1)
    for i in range(2):
        for k in range(4):
            at = i * 512 + k * W
            vp[2 * c + i, 8 + k : 9 + k, :] = fc_sum[:, at : at + W]

    for i in range(D // 256):
        cols = slice(i * 256, (i + 1) * 256)
        rs_c[:, cols] = dot_nt(pgh_s[...], fc_g[cols, :]).astype(BF16)
    h2g_sc.start()
    fc_rs.to_x()
    for i in range(D // 256):
        cols = slice(i * 256, (i + 1) * 256)
        rs_b[:, cols] = dot(act_s[...], out_g[:, cols]).astype(BF16)
    out_rs.to_z()

    grad_out = cot_ref[...].astype(F32)
    h2_grad = h2g_sc.finish()
    mid_grad = grad_out + norm_backward(h2_grad, normed2_s[...], inv2_s[...], vector(5))
    mid_all[span(c, T), :] = mid_grad.astype(BF16)
    mid_share.start()
    out_sc.start()
    midg_s[...] = mid_grad
    put_whole(4, jnp.sum(mid_grad, axis=0, keepdims=True))
    put_whole(5, jnp.sum(h2_grad * normed2_s[...], axis=0, keepdims=True))
    put_whole(6, jnp.sum(h2_grad, axis=0, keepdims=True))
    put_whole(7, jnp.sum(grad_out, axis=0, keepdims=True))
    mid_share.finish()
    ag_s[...] = dot_nt(mid_all[...], proj_g[...]).astype(BF16)

    for h in range(HEADS_HERE):
        cols = slice(h * HD, (h + 1) * HD)
        key_grad = [jnp.zeros((BLK, HD), F32) for _ in range(S // BLK)]
        value_grad = [jnp.zeros((BLK, HD), F32) for _ in range(S // BLK)]
        query_sum = jnp.zeros((1, HD), F32)
        for b in range(S // BLK):
            rows, upto = slice(b * BLK, (b + 1) * BLK), (b + 1) * BLK
            probs = p_s[h, rows, :upto]
            grads = ag_s[rows, cols]
            prob_grad = dot_nt(grads, v_s[:upto, cols])
            delta = jnp.sum(probs * prob_grad, axis=-1, keepdims=True)
            score_grad = (probs * (prob_grad - delta)).astype(BF16)
            half = probs.astype(BF16)
            query_grad = dot(score_grad, k_s[:upto, cols]) * HD ** (-0.5)
            query_sum = query_sum + jnp.sum(query_grad, axis=0, keepdims=True)
            dqkv_s[rows, h * HD : (h + 1) * HD] = query_grad.astype(BF16)
            key_part = dot_tn(score_grad, q_s[rows, cols])
            value_part = dot_tn(half, grads)
            for k in range(b + 1):
                key_grad[k] = key_grad[k] + key_part[k * BLK : (k + 1) * BLK, :]
                value_grad[k] = value_grad[k] + value_part[k * BLK : (k + 1) * BLK, :]
        value_sum = jnp.zeros((1, HD), F32)
        for k in range(S // BLK):
            rows = slice(k * BLK, (k + 1) * BLK)
            dqkv_s[rows, Q + h * HD : Q + (h + 1) * HD] = key_grad[k].astype(BF16)
            dqkv_s[rows, 2 * Q + h * HD : 2 * Q + (h + 1) * HD] = value_grad[k].astype(BF16)
            value_sum = value_sum + jnp.sum(value_grad[k], axis=0, keepdims=True)
        lane = slice((h % 2) * HD, (h % 2 + 1) * HD)
        vp[2 * c + h // 2, 2:3, lane] = query_sum
        vp[2 * c + h // 2, 3:4, lane] = value_sum

    for i in range(D // 256):
        cols = slice(i * 256, (i + 1) * 256)
        rs_d[:, cols] = dot_nt(dqkv_s[...], qkv_g[cols, :]).astype(BF16)
    h1g_sc.start()
    qkv_rs.to_x()
    xt_mid[...] = mid_all[...].T
    proj_rs.to_x()
    fc_rs.to_z()

    h1_grad = h1g_sc.finish()
    put_whole(0, jnp.sum(h1_grad * normed1_s[...], axis=0, keepdims=True))
    put_whole(1, jnp.sum(h1_grad, axis=0, keepdims=True))
    for j in range(NZ):
        send(vp.at[chunk(j, xo)], vxr.at[j], vec_xbase + j, x_dev)
    input_grad_out[...] = midg_s[...] + norm_backward(h1_grad, normed1_s[...], inv1_s[...], gain1)
    block_out[...] = (resid_s[...] + out_sc.finish() + vector(7)).astype(BF16)

    qkv_rs.to_z()
    proj_rs.to_z()
    for j in range(NZ):
        wait_recv(vxr.at[j], vec_xbase + j)
    for r in (1, 2, 3):
        zz = zat(r)
        vzs[r] = vp[chunk(zz, x)] + vxr[zz]
        send(vzs.at[r], vzr.at[r], vec_zbase + r - 1, z_dev(r))
    g_out[...] = out_rs.total().T
    g_fc[...] = fc_rs.total()
    own = vp[chunk(z, x)] + vxr[z]
    for r in (1, 2, 3):
        wait_recv(vzr.at[r], vec_zbase + r - 1)
        own = own + vzr[r]
    vcs[...] = own
    for r in (1, 2, 3):
        send(vcs, vcr.at[c], vec_cbase + r - 1, c_dev(r))
    vcr[c] = own
    g_qkv[...] = qkv_rs.total()
    g_proj[...] = proj_rs.total().T
    for r in (1, 2, 3):
        wait_recv(vcr.at[(c + NC - r) % NC], vec_cbase + r - 1)
    vec_out[...] = vcr[0] + vcr[1] + vcr[2] + vcr[3]

    for copy in sends:
        copy.wait_send()


def fused_body(
    block_input, segment_ids, ln1_gain, ln1_bias, qkv_weight, query_bias, value_bias, proj_weight, proj_bias,
    ln2_gain, ln2_bias, fc_weight, fc_bias, out_weight, out_bias, cotangent,
):
    vec = jnp.concatenate(
        [ln1_gain, ln1_bias, query_bias, value_bias, proj_bias, ln2_gain, ln2_bias, out_bias, fc_bias,
         jnp.zeros((4 * W,), BF16)]
    ).reshape(VEC_ROWS, W)
    vmem = pl.BlockSpec(memory_space=pltpu.VMEM)

    def buf(*shape, kind=BF16):
        return pltpu.VMEM(shape, kind)

    widths = (3 * Q, Q, U, U)
    scratch = [
        buf(NDP, VEC_ROWS, W), buf(D, 3 * Q), buf(Q, D), buf(D, U), buf(U, D),
        *[buf(S, D) for _ in range(4)], *[buf(D, S) for _ in range(4)],
        buf(S, Q), buf(S, Q), buf(S, Q), buf(S, Q), buf(HEADS_HERE, S, S, kind=F32), buf(S, S, kind=F32),
        buf(S, U), buf(S, U, kind=F32), buf(S, U), buf(S, Q), buf(S, 3 * Q),
        buf(T, D, kind=F32), buf(T, D, kind=F32), buf(T, 1, kind=F32), buf(T, D, kind=F32), buf(T, 1, kind=F32),
        buf(T, D, kind=F32),
        *[buf(S, D) for _ in range(4)], *[buf(NC, T, D) for _ in range(4)],
        *[buf(NZ, W, n) for _ in range(4) for n in widths],
        buf(NDP, VEC_ROWS, W, kind=F32), buf(NZ, VEC_ROWS, W, kind=F32), buf(NZ, VEC_ROWS, W, kind=F32),
        buf(NZ, VEC_ROWS, W, kind=F32), buf(VEC_ROWS, W, kind=F32), buf(NC, VEC_ROWS, W, kind=F32),
        pltpu.SemaphoreType.DMA((112,)), pltpu.SemaphoreType.DMA((112,)),
    ]
    outs = pl.pallas_call(
        fused_kernel,
        out_shape=[
            jax.ShapeDtypeStruct((T, D), BF16),
            jax.ShapeDtypeStruct((T, D), F32),
            jax.ShapeDtypeStruct((W, 3 * Q), F32),
            jax.ShapeDtypeStruct((Q, W), F32),
            jax.ShapeDtypeStruct((W, U), F32),
            jax.ShapeDtypeStruct((U, W), F32),
            jax.ShapeDtypeStruct((VEC_ROWS, W), F32),
        ],
        in_specs=[vmem] * 9,
        out_specs=[vmem] * 7,
        scratch_shapes=scratch,
        compiler_params=pltpu.CompilerParams(
            collective_id=0, has_side_effects=True, vmem_limit_bytes=60 * 1024 * 1024
        ),
    )(
        block_input[0], cotangent[0], segment_ids, segment_ids.reshape(S, 1), vec,
        qkv_weight.reshape(W, 3 * Q), proj_weight, fc_weight, out_weight,
    )
    block_output, input_grad, qkv_grad, proj_grad, fc_grad, out_grad, vecs = outs
    return (
        block_output[None], input_grad[None], vecs[0], vecs[1], qkv_grad.reshape(W, 3, Q), vecs[2], vecs[3],
        proj_grad, vecs[4], vecs[5], vecs[6], fc_grad, vecs[8:12].reshape(-1), out_grad, vecs[7],
    )


def solution(mesh):
    return jax.shard_map(
        fused_body if fits(mesh) else body,
        mesh=mesh,
        in_specs=(
            P("dp", "ctx", None),
            P("dp", None),
            P("dp"),
            P("dp"),
            P("dp", None, "ctx"),
            P("dp"),
            P("dp"),
            P("ctx", "dp"),
            P("dp"),
            P("dp"),
            P("dp"),
            P("dp", "ctx"),
            P("dp"),
            P("ctx", "dp"),
            P("dp"),
            P("dp", "ctx", None),
        ),
        out_specs=(
            P("dp", "ctx", None),
            P("dp", "ctx", None),
            P("dp"),
            P("dp"),
            P("dp", None, "ctx"),
            P("dp"),
            P("dp"),
            P("ctx", "dp"),
            P("dp"),
            P("dp"),
            P("dp"),
            P("dp", "ctx"),
            P("dp"),
            P("ctx", "dp"),
            P("dp"),
        ),
        check_vma=False,
    )
```

```python
import functools
import jax
import jax.numpy as jnp
from jax import lax
from jax.experimental import pallas as pl
from jax.experimental.pallas import tpu as pltpu
from jax.sharding import PartitionSpec as P

D = 1024
HD = 64
FF = 4096


NORM_EPS = 1e-05
GELU_ROOT = 0.7978845608028654
GELU_CUBE = 0.044715
MASK_VALUE = -1e30


def norm_forward(residual):
    row_mean = jnp.mean(residual, axis=-1, keepdims=True)
    centered = residual - row_mean
    row_var = jnp.mean(centered * centered, axis=-1, keepdims=True)
    inv_std = lax.rsqrt(row_var + NORM_EPS)
    return (centered * inv_std, inv_std)


def norm_backward(grad_in, normed, inv_std, gain):
    scaled = grad_in * gain
    mean_scaled = jnp.mean(scaled, axis=-1, keepdims=True)
    mean_cross = jnp.mean(scaled * normed, axis=-1, keepdims=True)
    return inv_std * (scaled - mean_scaled - normed * mean_cross)


def gelu_pair(pre_act):
    inner_arg = GELU_ROOT * (pre_act + GELU_CUBE * pre_act * pre_act * pre_act)
    tangent = jnp.tanh(inner_arg)
    activated = 0.5 * pre_act * (1.0 + tangent)
    gelu_slope = 0.5 * (1.0 + tangent) + 0.5 * pre_act * (1.0 - tangent * tangent) * GELU_ROOT * (
        1.0 + 3.0 * GELU_CUBE * pre_act * pre_act
    )
    return (activated, gelu_slope)


def masked_scores(query_heads, key_heads, allowed):
    raw_scores = jnp.einsum(
        "qhd,khd->hqk", query_heads, key_heads, preferred_element_type=jnp.float32
    ) * HD ** (-0.5)
    return jnp.where(allowed[None], raw_scores, MASK_VALUE)


def attend(query_heads, key_heads, value_heads, allowed):
    scores = masked_scores(query_heads, key_heads, allowed)
    top_score = jnp.max(scores, axis=-1, keepdims=True)
    log_total = top_score + jnp.log(jnp.sum(jnp.exp(scores - top_score), axis=-1, keepdims=True))
    attn_probs = jnp.where(allowed[None], jnp.exp(scores - log_total), 0.0)
    probs_half = attn_probs.astype(jnp.bfloat16)
    attended = jnp.einsum(
        "hqk,khd->qhd", probs_half, value_heads, preferred_element_type=jnp.float32
    )
    return (attended.reshape(query_heads.shape[0], -1).astype(jnp.bfloat16), log_total)


def attend_back(query_heads, key_heads, value_heads, allowed, log_total, grad_heads):
    scores = masked_scores(query_heads, key_heads, allowed)
    attn_probs = jnp.where(allowed[None], jnp.exp(scores - log_total), 0.0)
    probs_half = attn_probs.astype(jnp.bfloat16)
    prob_grad = jnp.einsum(
        "qhd,khd->hqk", grad_heads, value_heads, preferred_element_type=jnp.float32
    )
    value_part = jnp.einsum(
        "hqk,qhd->khd", probs_half, grad_heads, preferred_element_type=jnp.float32
    )
    delta_rows = jnp.sum(attn_probs * prob_grad, axis=-1, keepdims=True)
    score_grad = (attn_probs * (prob_grad - delta_rows) * HD ** (-0.5)).astype(jnp.bfloat16)
    query_grad = jnp.einsum(
        "hqk,khd->qhd", score_grad, key_heads, preferred_element_type=jnp.float32
    )
    key_part = jnp.einsum(
        "hqk,qhd->khd", score_grad, query_heads, preferred_element_type=jnp.float32
    )
    key_count = key_heads.shape[0]
    return (
        query_grad.reshape(query_heads.shape[0], -1),
        key_part.reshape(key_count, -1),
        value_part.reshape(key_count, -1),
    )


def place_part(part, whole_len, start):
    return lax.dynamic_update_slice_in_dim(jnp.zeros((whole_len,), jnp.float32), part, start, 0)


def body(
    block_input,
    segment_ids,
    ln1_gain,
    ln1_bias,
    qkv_weight,
    query_bias,
    value_bias,
    proj_weight,
    proj_bias,
    ln2_gain,
    ln2_bias,
    fc_weight,
    fc_bias,
    out_weight,
    out_bias,
    cotangent,
):
    tokens = block_input[0]
    seg_whole = segment_ids[0]
    grad_rows = cotangent[0]
    seq_length = seg_whole.shape[0]
    ctx_rank = lax.axis_index("ctx")
    key_pos = jnp.arange(seq_length, dtype=jnp.int32)
    resid_in = tokens.astype(jnp.float32)
    normed_one, inv_one = norm_forward(resid_in)
    grad_out = grad_rows.astype(jnp.float32)
    out_shift_grad = jnp.sum(grad_out, axis=0)
    vectors = lax.all_gather(
        jnp.concatenate(
            [ln1_gain, ln1_bias, query_bias, value_bias, proj_bias, ln2_gain, ln2_bias, out_bias, fc_bias]
        ),
        "dp",
        axis=0,
    )
    slice_len = ln1_gain.shape[0]
    dp_size = vectors.shape[0]
    ff_whole = fc_bias.shape[0] * dp_size

    def vector(at):
        return vectors[:, at * slice_len : (at + 1) * slice_len].astype(jnp.float32).reshape(-1)

    qkv_cols = lax.all_gather(qkv_weight, "dp", axis=0, tiled=True).reshape(D, -1)
    proj_rows = lax.all_gather(proj_weight, "dp", axis=1, tiled=True)
    fc_cols = lax.all_gather(fc_weight, "dp", axis=0, tiled=True)
    out_rows = lax.all_gather(out_weight, "dp", axis=1, tiled=True)
    quarter = proj_rows.shape[0]
    unit_part = fc_cols.shape[1]
    gain_first = vector(0)
    shift_first = vector(1)
    query_shift = lax.dynamic_slice_in_dim(vector(2), ctx_rank * quarter, quarter)
    value_shift = lax.dynamic_slice_in_dim(vector(3), ctx_rank * quarter, quarter)
    proj_shift = vector(4)
    gain_second = vector(5)
    shift_second = vector(6)
    out_shift = vector(7)
    fc_shift = lax.dynamic_slice_in_dim(
        vectors[:, 8 * slice_len :].astype(jnp.float32).reshape(-1), ctx_rank * unit_part, unit_part
    )
    local_heads = quarter // HD
    allowed = (key_pos[:, None] >= key_pos[None, :]) & (seg_whole[:, None] == seg_whole[None, :])
    hidden_one = (normed_one * gain_first + shift_first).astype(jnp.bfloat16)
    hidden_all, grad_all = (
        lax.all_gather(hidden_one, "ctx", axis=0, tiled=True),
        lax.all_gather(grad_rows, "ctx", axis=0, tiled=True),
    )
    qkv_out = jnp.dot(hidden_all, qkv_cols, preferred_element_type=jnp.float32)
    queries = (qkv_out[:, :quarter] + query_shift).astype(jnp.bfloat16)
    keys_here = qkv_out[:, quarter : 2 * quarter].astype(jnp.bfloat16)
    values_here = (qkv_out[:, 2 * quarter :] + value_shift).astype(jnp.bfloat16)
    query_heads = queries.reshape(seq_length, local_heads, HD)
    key_heads = keys_here.reshape(seq_length, local_heads, HD)
    value_heads = values_here.reshape(seq_length, local_heads, HD)
    attended, log_total = attend(query_heads, key_heads, value_heads, allowed)
    resid_mid = (
        resid_in
        + lax.psum_scatter(
            jnp.dot(attended, proj_rows, preferred_element_type=jnp.float32).astype(jnp.bfloat16),
            "ctx",
            scatter_dimension=0,
            tiled=True,
        ).astype(jnp.float32)
        + proj_shift
    )
    normed_two, inv_two = norm_forward(resid_mid)
    hidden_two = (normed_two * gain_second + shift_second).astype(jnp.bfloat16)
    hidden_two_all = lax.all_gather(hidden_two, "ctx", axis=0, tiled=True)
    pre_act = jnp.dot(hidden_two_all, fc_cols, preferred_element_type=jnp.float32) + fc_shift
    activated, gelu_slope = gelu_pair(pre_act)
    activated = activated.astype(jnp.bfloat16)
    block_output = (
        resid_mid
        + lax.psum_scatter(
            jnp.dot(activated, out_rows, preferred_element_type=jnp.float32).astype(jnp.bfloat16),
            "ctx",
            scatter_dimension=0,
            tiled=True,
        ).astype(jnp.float32)
        + out_shift
    ).astype(jnp.bfloat16)
    out_weight_grad = jnp.dot(activated.T, grad_all, preferred_element_type=jnp.float32)
    pre_grad = jnp.dot(grad_all, out_rows.T, preferred_element_type=jnp.float32) * gelu_slope
    fc_shift_grad = place_part(jnp.sum(pre_grad, axis=0), ff_whole, ctx_rank * unit_part)
    pre_grad_half = pre_grad.astype(jnp.bfloat16)
    fc_weight_grad = jnp.dot(hidden_two_all.T, pre_grad_half, preferred_element_type=jnp.float32)
    hidden_two_grad = lax.psum_scatter(
        jnp.dot(pre_grad_half, fc_cols.T, preferred_element_type=jnp.float32).astype(jnp.bfloat16),
        "ctx",
        scatter_dimension=0,
        tiled=True,
    ).astype(jnp.float32)
    gain_second_grad = jnp.sum(hidden_two_grad * normed_two, axis=0)
    shift_second_grad = jnp.sum(hidden_two_grad, axis=0)
    mid_grad = grad_out + norm_backward(hidden_two_grad, normed_two, inv_two, gain_second)
    proj_shift_grad = jnp.sum(mid_grad, axis=0)
    mid_grad_half = mid_grad.astype(jnp.bfloat16)
    mid_all = lax.all_gather(mid_grad_half, "ctx", axis=0, tiled=True)
    proj_weight_grad = jnp.dot(attended.T, mid_all, preferred_element_type=jnp.float32)
    attended_grad = jnp.dot(mid_all, proj_rows.T, preferred_element_type=jnp.float32).astype(
        jnp.bfloat16
    )
    grad_heads = attended_grad.reshape(seq_length, local_heads, HD)
    query_grad, key_grad, value_grad = attend_back(
        query_heads, key_heads, value_heads, allowed, log_total, grad_heads
    )
    query_shift_grad = place_part(jnp.sum(query_grad, axis=0), D, ctx_rank * quarter)
    value_shift_grad = place_part(jnp.sum(value_grad, axis=0), D, ctx_rank * quarter)
    qkv_grad = jnp.concatenate([query_grad, key_grad, value_grad], axis=1).astype(jnp.bfloat16)
    qkv_weight_grad = jnp.dot(hidden_all.T, qkv_grad, preferred_element_type=jnp.float32).reshape(
        D, 3, quarter
    )
    hidden_one_grad = lax.psum_scatter(
        jnp.dot(qkv_grad, qkv_cols.T, preferred_element_type=jnp.float32).astype(jnp.bfloat16),
        "ctx",
        scatter_dimension=0,
        tiled=True,
    ).astype(jnp.float32)
    gain_first_grad = jnp.sum(hidden_one_grad * normed_one, axis=0)
    shift_first_grad = jnp.sum(hidden_one_grad, axis=0)
    input_grad = mid_grad + norm_backward(hidden_one_grad, normed_one, inv_one, gain_first)
    half = jnp.bfloat16
    matrix_sums = (
        lax.psum_scatter(qkv_weight_grad.astype(half), "dp", scatter_dimension=0, tiled=True),
        lax.psum_scatter(proj_weight_grad.astype(half), "dp", scatter_dimension=1, tiled=True),
        lax.psum_scatter(fc_weight_grad.astype(half), "dp", scatter_dimension=0, tiled=True),
        lax.psum_scatter(out_weight_grad.astype(half), "dp", scatter_dimension=1, tiled=True),
    )
    matrix_sums = tuple(m.astype(jnp.float32) for m in matrix_sums)
    packed = jnp.concatenate(
        [
            v.reshape(dp_size, -1)
            for v in (
                gain_first_grad,
                shift_first_grad,
                query_shift_grad,
                value_shift_grad,
                proj_shift_grad,
                gain_second_grad,
                shift_second_grad,
                out_shift_grad,
                fc_shift_grad,
            )
        ],
        axis=1,
    )
    packed = lax.psum(packed, ("dp", "ctx"))
    mine = lax.dynamic_index_in_dim(packed, lax.axis_index("dp"), 0, keepdims=False)
    order = (0, 1, 2, 3, 4, 5, 6, 8, 7)
    pieces = [mine[i * slice_len : (i + 1) * slice_len] for i in range(8)] + [mine[8 * slice_len :]]
    vector_sums = tuple(pieces[i] for i in order)
    return (
        block_output[None],
        input_grad[None],
        vector_sums[0],
        vector_sums[1],
        matrix_sums[0],
        vector_sums[2],
        vector_sums[3],
        matrix_sums[1],
        vector_sums[4],
        vector_sums[5],
        vector_sums[6],
        matrix_sums[2],
        vector_sums[7],
        matrix_sums[3],
        vector_sums[8],
    )


NX = 2
NZ = 4
NDP = NX * NZ
NC = 4
T = 128
S = NC * T
W = 128
Q = D // NC
U = FF // NC
HEADS_HERE = Q // HD
BLK = 256
MESH = pl.DeviceIdType.MESH
F32 = jnp.float32
BF16 = jnp.bfloat16
VEC_ROWS = 16


def fits(mesh):
    return mesh.shape["dp"] == NDP and mesh.shape["ctx"] == NC


def dot(a, b):
    return jnp.dot(a, b, preferred_element_type=F32)


def dot_nt(a, b):
    return lax.dot_general(a, b, (((1,), (1,)), ((), ())), preferred_element_type=F32)


def dot_tn(a, b):
    return lax.dot_general(a, b, (((0,), (0,)), ((), ())), preferred_element_type=F32)


def fused_kernel(
    x_hbm, cot_hbm, seg_hbm, qkv_hbm, proj_hbm, fc_hbm, outw_hbm,
    v0, v1, v2, v3, v4, v5, v6, v7, v8,
    block_out, input_grad_out, g_qkv, g_proj, g_fc, g_out, vec_out,
    x_ref, seg_ref, n0, n1, n2, n3, n4, n5, n6, n7, n8, lsem,
    vec_g, qkv_g, proj_g, fc_g, out_g,
    h_all, cot_all, h2_all, mid_all, xt_h, xt_cot, xt_h2, xt_mid,
    q_s, k_s, v_s, att_s, p_s, bias_s, act_s, slope_s, pgh_s, ag_s, dqkv_s,
    resid_s, normed1_s, inv1_s, normed2_s, inv2_s, midg_s,
    rs_a, rs_b, rs_c, rs_d, rr_a, rr_b, rr_c, rr_d,
    xs_qkv, xs_proj, xs_fc, xs_out, xr_qkv, xr_proj, xr_fc, xr_out,
    zs_qkv, zs_proj, zs_fc, zs_out, zr_qkv, zr_proj, zr_fc, zr_out,
    vp, vxr, vzs, vzr, vcs, vcr,
    ssem, rsem,
):
    dp = lax.axis_index("dp")
    c = lax.axis_index("ctx")
    z = dp // NX
    x = dp % NX
    xo = 1 - x

    def zat(r):
        return (z + r) % NZ

    def chunk(zz, xx):
        return zz * NX + xx

    def span(i, n):
        return pl.ds(pl.multiple_of(i * n, n), n)

    counter = [0]
    sends = []
    guarded = []

    def sem_block(n):
        base = counter[0]
        counter[0] += n
        return base

    def remote(src, dst, sem, dev):
        return pltpu.make_async_remote_copy(
            src_ref=src, dst_ref=dst, send_sem=ssem.at[sem], recv_sem=rsem.at[sem],
            device_id=dev, device_id_type=MESH,
        )

    def send(src, dst, sem, dev):
        copy = remote(src, dst, sem, dev)
        copy.start()
        sends.append(copy)

    x_dev = (chunk(z, xo), c)

    def z_dev(r):
        return (chunk(zat(r), x), c)

    def c_dev(r):
        return (dp, (c + r) % NC)

    loads = []

    def load(src, dst):
        copy = pltpu.make_async_copy(src, dst, lsem.at[len(loads)])
        copy.start()
        loads.append(copy)

    def wait_recv(dst, sem):
        remote(dst, dst, sem, x_dev).wait_recv()

    def send_if(cond, src, dst, sem, dev):
        copy = remote(src, dst, sem, dev)

        @pl.when(cond)
        def _():
            copy.start()

        guarded.append((cond, copy))

    def z_next(up):
        return (chunk(z + 1 if up else z - 1, x), c)

    def has_next(up):
        return z < NZ - 1 if up else z > 0

    class Gather:
        def __init__(self, slot):
            self.slot = slot
            self.zbase, self.xbase = sem_block(2 * (NZ - 1)), sem_block(2 * (NZ - 1) + 1)

        def start_z(self):
            here = self.slot(dp)
            for up in (True, False):
                send_if(has_next(up), here, here, self.zbase + (0 if up else NZ - 1), z_next(up))

        def start_x(self):
            here = self.slot(dp)
            send(here, here, self.xbase + 2 * (NZ - 1), x_dev)

        def arrives(self, up, k):
            return (z >= k) if up else (z + k < NZ)

        def step(self, k):
            for up in (True, False):
                at = (0 if up else NZ - 1) + k - 1
                here = self.slot(chunk(z - k if up else z + k, x))

                @pl.when(self.arrives(up, k))
                def _():
                    wait_recv(here, self.zbase + at)

                if k < NZ - 1:
                    send_if(self.arrives(up, k) & has_next(up), here, here, self.zbase + at + 1, z_next(up))
                send_if(self.arrives(up, k), here, here, self.xbase + at, x_dev)

        def finish(self):
            wait_recv(self.slot(chunk(z, xo)), self.xbase + 2 * (NZ - 1))
            for k in range(1, NZ):
                for up in (True, False):

                    @pl.when(self.arrives(up, k))
                    def _():
                        wait_recv(
                            self.slot(chunk(z - k if up else z + k, xo)),
                            self.xbase + (0 if up else NZ - 1) + k - 1,
                        )

    def rows_slot(buf):
        return lambda d: buf.at[span(d, W)]

    def cols_slot(buf):
        return lambda d: buf.at[:, span(d, W)]

    vec_base = sem_block(NDP - 1)
    qkv_ag = Gather(rows_slot(qkv_g))
    proj_ag = Gather(cols_slot(proj_g))
    fc_ag = Gather(rows_slot(fc_g))
    out_ag = Gather(cols_slot(out_g))

    class Reduce:
        def __init__(self, left, right, xs, xr, zs, zr, width):
            self.left, self.right, self.width = left, right, width
            self.xs, self.xr, self.zs, self.zr = xs, xr, zs, zr
            self.xbase, self.zbase = sem_block(NZ), sem_block(NZ - 1)

        def part(self, d):
            return dot(self.left[span(d, W), :], self.right[...])

        def to_x(self):
            for r in (2, 1, 3, 0):
                j = zat(r)
                self.xs[j] = self.part(chunk(j, xo)).astype(BF16)
                send(self.xs.at[j], self.xr.at[j], self.xbase + j, x_dev)

        def to_z(self):
            for r in (2, 1, 3):
                zz = zat(r)
                wait_recv(self.xr.at[zz], self.xbase + zz)
                total = self.part(chunk(zz, x)) + self.xr[zz].astype(F32)
                self.zs[r] = total.astype(BF16)
                send(self.zs.at[r], self.zr.at[r], self.zbase + r - 1, z_dev(r))

        def total(self):
            wait_recv(self.xr.at[z], self.xbase + z)
            own = self.part(chunk(z, x)) + self.xr[z].astype(F32)
            for r in (1, 3, 2):
                wait_recv(self.zr.at[r], self.zbase + r - 1)
                own = own + self.zr[r].astype(F32)
            return own

    out_rs = Reduce(xt_cot, act_s, xs_out, xr_out, zs_out, zr_out, U)
    fc_rs = Reduce(xt_h2, pgh_s, xs_fc, xr_fc, zs_fc, zr_fc, U)
    proj_rs = Reduce(xt_mid, att_s, xs_proj, xr_proj, zs_proj, zr_proj, Q)
    qkv_rs = Reduce(xt_h, dqkv_s, xs_qkv, xr_qkv, zs_qkv, zr_qkv, 3 * Q)
    vec_xbase, vec_zbase, vec_cbase = sem_block(NZ), sem_block(NZ), sem_block(NC)

    class Share:
        def __init__(self, buf):
            self.buf, self.base = buf, sem_block(NC - 1)

        def start(self):
            here = self.buf.at[span(c, T)]
            for r in (2, 1, 3):
                send(here, here, self.base + r - 1, c_dev(r))

        def finish(self):
            for r in (1, 2, 3):
                wait_recv(self.buf.at[span((c + NC - r) % NC, T)], self.base + r - 1)

    class Scatter:
        def __init__(self, full, got):
            self.full, self.got, self.base = full, got, sem_block(NC - 1)

        def start(self):
            for r in (2, 1, 3):
                send(self.full.at[span((c + r) % NC, T)], self.got.at[r], self.base + r - 1, c_dev(r))

        def finish(self):
            total = self.full[span(c, T), :].astype(F32)
            for r in (1, 2, 3):
                wait_recv(self.got.at[r], self.base + r - 1)
                total = total + self.got[r].astype(F32)
            return total

    h_share, cot_share, h2_share, mid_share = Share(h_all), Share(cot_all), Share(h2_all), Share(mid_all)
    proj_sc, out_sc, h2g_sc, h1g_sc = (
        Scatter(rs_a, rr_a), Scatter(rs_b, rr_b), Scatter(rs_c, rr_c), Scatter(rs_d, rr_d)
    )

    vec_in = (n0, n1, n2, n3, n4, n5, n6, n7, n8)
    for src, dst in zip((v0, v1, v2, v3, v4, v5, v6, v7, v8), vec_in):
        load(src, dst)
    for j in range(3):
        load(qkv_hbm.at[j], qkv_g.at[span(dp, W), j * Q : (j + 1) * Q])
    load(proj_hbm, proj_g.at[:, span(dp, W)])
    load(x_hbm, x_ref)
    load(seg_hbm, seg_ref)
    load(cot_hbm, cot_all.at[span(c, T)])
    load(fc_hbm, fc_g.at[span(dp, W)])
    load(outw_hbm, out_g.at[:, span(dp, W)])
    barrier = pltpu.get_barrier_semaphore()
    peers = [((dp + r) % NDP, c) for r in range(1, NDP)] + [c_dev(r) for r in (1, 2, 3)]
    for dev in peers:
        pl.semaphore_signal(barrier, inc=1, device_id=dev, device_id_type=MESH)
    pl.semaphore_wait(barrier, len(peers))
    for copy in loads:
        copy.wait()
    vec_g[dp] = jnp.concatenate(
        [v[...].astype(F32) for v in vec_in] + [jnp.zeros((4, W), F32)], axis=0
    ).astype(BF16)
    for r in range(1, NDP):
        send(vec_g.at[dp], vec_g.at[dp], vec_base + r - 1, ((dp + r) % NDP, c))
    qkv_ag.start_z()
    qkv_ag.start_x()
    proj_ag.start_z()
    proj_ag.start_x()
    fc_ag.start_x()
    resid_in = x_ref[...].astype(F32)
    normed, inv = norm_forward(resid_in)
    normed1_s[...] = normed
    inv1_s[...] = inv
    key_pos = lax.broadcasted_iota(jnp.int32, (S, S), 1)
    query_pos = lax.broadcasted_iota(jnp.int32, (S, S), 0)
    seg_row = seg_ref[...].astype(F32)
    seg_down = jnp.broadcast_to(seg_row, (W, S)).T[:, :1]
    allowed = (query_pos >= key_pos) & (seg_down == seg_row)
    bias_s[...] = jnp.where(allowed, 0.0, MASK_VALUE)
    vp[...] = jnp.zeros_like(vp)

    for r in range(1, NDP):
        wait_recv(vec_g.at[(dp + NDP - r) % NDP], vec_base + r - 1)
    vectors = vec_g[...].astype(F32)

    def vector(row):
        return jnp.concatenate([vectors[d, row : row + 1, :] for d in range(NDP)], axis=1)

    gain1, shift1 = vector(0), vector(1)
    h_all[span(c, T), :] = (normed * gain1 + shift1).astype(BF16)
    h_share.start()
    cot_share.start()

    qkv_ag.step(1)
    fc_ag.start_z()
    qkv_ag.step(2)
    qkv_ag.step(3)
    for k in (1, 2, 3):
        proj_ag.step(k)
    out_ag.start_x()
    h_share.finish()
    qkv_ag.finish()

    def quarter_vector(row):
        first = vec_g[2 * c].astype(F32)[row : row + 1, :]
        second = vec_g[2 * c + 1].astype(F32)[row : row + 1, :]
        return jnp.concatenate([first, second], axis=1)

    q_s[...] = ((dot(h_all[...], qkv_g[:, :Q]) + quarter_vector(2)).astype(BF16).astype(F32) * HD ** (-0.5)).astype(BF16)
    k_s[...] = dot(h_all[...], qkv_g[:, Q : 2 * Q]).astype(BF16)
    v_s[...] = (dot(h_all[...], qkv_g[:, 2 * Q :]) + quarter_vector(3)).astype(BF16)


    for h in range(HEADS_HERE):
        cols = slice(h * HD, (h + 1) * HD)
        for b in range(S // BLK):
            rows, upto = slice(b * BLK, (b + 1) * BLK), (b + 1) * BLK
            scores = dot_nt(q_s[rows, cols], k_s[:upto, cols]) + bias_s[rows, :upto]
            top = jnp.max(scores, axis=-1, keepdims=True)
            weights = jnp.exp(scores - top)
            probs = weights * (1.0 / jnp.sum(weights, axis=-1, keepdims=True))
            p_s[h, rows, :upto] = probs
            att_s[rows, cols] = dot(probs.astype(BF16), v_s[:upto, cols]).astype(BF16)

    proj_ag.finish()
    for i in range(D // 256):
        cols = slice(i * 256, (i + 1) * 256)
        rs_a[:, cols] = dot(att_s[...], proj_g[:, cols]).astype(BF16)
    proj_sc.start()
    xt_h[...] = h_all[...].T
    cot_share.finish()
    xt_cot[...] = cot_all[...].T
    fc_ag.step(1)
    out_ag.start_z()
    fc_ag.step(2)
    fc_ag.step(3)

    resid_mid = x_ref[...].astype(F32) + proj_sc.finish() + vector(4)
    resid_s[...] = resid_mid
    normed, inv = norm_forward(resid_mid)
    normed2_s[...] = normed
    inv2_s[...] = inv
    h2_all[span(c, T), :] = (normed * vector(5) + vector(6)).astype(BF16)
    h2_share.start()
    for k in (1, 2, 3):
        out_ag.step(k)
    h2_share.finish()
    fc_ag.finish()

    def fc_vector():
        pieces = []
        for i in range(2):
            block = vec_g[2 * c + i].astype(F32)
            pieces += [block[8 + k : 9 + k, :] for k in range(4)]
        return jnp.concatenate(pieces, axis=1)

    fc_shift = fc_vector()
    for i in range(U // 256):
        cols = slice(i * 256, (i + 1) * 256)
        activated, slope = gelu_pair(dot(h2_all[...], fc_g[:, cols]) + fc_shift[:, cols])
        act_s[:, cols] = activated.astype(BF16)
        slope_s[:, cols] = slope
    xt_h2[...] = h2_all[...].T

    out_rs.to_x()
    out_ag.finish()

    def put_quarter(row, total):
        for i in range(2):
            vp[2 * c + i, row : row + 1, :] = total[:, i * W : (i + 1) * W]

    def put_whole(row, total):
        for d in range(NDP):
            vp[d, row : row + 1, :] = total[:, d * W : (d + 1) * W]

    sums = []
    for i in range(U // 256):
        cols = slice(i * 256, (i + 1) * 256)
        pre_grad = dot_nt(cot_all[...], out_g[cols, :]) * slope_s[:, cols]
        sums.append(jnp.sum(pre_grad, axis=0, keepdims=True))
        pgh_s[:, cols] = pre_grad.astype(BF16)
    fc_sum = jnp.concatenate(sums, axis=1)
    for i in range(2):
        for k in range(4):
            at = i * 512 + k * W
            vp[2 * c + i, 8 + k : 9 + k, :] = fc_sum[:, at : at + W]

    for i in range(D // 256):
        cols = slice(i * 256, (i + 1) * 256)
        rs_c[:, cols] = dot_nt(pgh_s[...], fc_g[cols, :]).astype(BF16)
    h2g_sc.start()
    fc_rs.to_x()
    for i in range(D // 256):
        cols = slice(i * 256, (i + 1) * 256)
        rs_b[:, cols] = dot(act_s[...], out_g[:, cols]).astype(BF16)

    grad_out = cot_all[span(c, T), :].astype(F32)
    h2_grad = h2g_sc.finish()
    mid_grad = grad_out + norm_backward(h2_grad, normed2_s[...], inv2_s[...], vector(5))
    mid_all[span(c, T), :] = mid_grad.astype(BF16)
    mid_share.start()
    out_sc.start()
    midg_s[...] = mid_grad
    put_whole(4, jnp.sum(mid_grad, axis=0, keepdims=True))
    put_whole(5, jnp.sum(h2_grad * normed2_s[...], axis=0, keepdims=True))
    put_whole(6, jnp.sum(h2_grad, axis=0, keepdims=True))
    put_whole(7, jnp.sum(grad_out, axis=0, keepdims=True))
    out_rs.to_z()
    mid_share.finish()
    ag_s[...] = dot_nt(mid_all[...], proj_g[...]).astype(BF16)

    for h in range(HEADS_HERE):
        cols = slice(h * HD, (h + 1) * HD)
        key_grad = [jnp.zeros((BLK, HD), F32) for _ in range(S // BLK)]
        value_grad = [jnp.zeros((BLK, HD), F32) for _ in range(S // BLK)]
        query_sum = jnp.zeros((1, HD), F32)
        for b in range(S // BLK):
            rows, upto = slice(b * BLK, (b + 1) * BLK), (b + 1) * BLK
            probs = p_s[h, rows, :upto]
            grads = ag_s[rows, cols]
            prob_grad = dot_nt(grads, v_s[:upto, cols])
            delta = jnp.sum(probs * prob_grad, axis=-1, keepdims=True)
            score_grad = (probs * (prob_grad - delta)).astype(BF16)
            half = probs.astype(BF16)
            query_grad = dot(score_grad, k_s[:upto, cols]) * HD ** (-0.5)
            query_sum = query_sum + jnp.sum(query_grad, axis=0, keepdims=True)
            dqkv_s[rows, h * HD : (h + 1) * HD] = query_grad.astype(BF16)
            key_part = dot_tn(score_grad, q_s[rows, cols])
            value_part = dot_tn(half, grads)
            for k in range(b + 1):
                key_grad[k] = key_grad[k] + key_part[k * BLK : (k + 1) * BLK, :]
                value_grad[k] = value_grad[k] + value_part[k * BLK : (k + 1) * BLK, :]
        value_sum = jnp.zeros((1, HD), F32)
        for k in range(S // BLK):
            rows = slice(k * BLK, (k + 1) * BLK)
            dqkv_s[rows, Q + h * HD : Q + (h + 1) * HD] = key_grad[k].astype(BF16)
            dqkv_s[rows, 2 * Q + h * HD : 2 * Q + (h + 1) * HD] = value_grad[k].astype(BF16)
            value_sum = value_sum + jnp.sum(value_grad[k], axis=0, keepdims=True)
        lane = slice((h % 2) * HD, (h % 2 + 1) * HD)
        vp[2 * c + h // 2, 2:3, lane] = query_sum
        vp[2 * c + h // 2, 3:4, lane] = value_sum

    for i in range(D // 256):
        cols = slice(i * 256, (i + 1) * 256)
        rs_d[:, cols] = dot_nt(dqkv_s[...], qkv_g[cols, :]).astype(BF16)
    h1g_sc.start()
    qkv_rs.to_x()
    xt_mid[...] = mid_all[...].T
    proj_rs.to_x()
    fc_rs.to_z()

    h1_grad = h1g_sc.finish()
    put_whole(0, jnp.sum(h1_grad * normed1_s[...], axis=0, keepdims=True))
    put_whole(1, jnp.sum(h1_grad, axis=0, keepdims=True))
    for j in range(NZ):
        send(vp.at[chunk(j, xo)], vxr.at[j], vec_xbase + j, x_dev)
    input_grad_out[...] = midg_s[...] + norm_backward(h1_grad, normed1_s[...], inv1_s[...], gain1)
    block_out[...] = (resid_s[...] + out_sc.finish() + vector(7)).astype(BF16)

    qkv_rs.to_z()
    proj_rs.to_z()
    for j in range(NZ):
        wait_recv(vxr.at[j], vec_xbase + j)
    for r in (1, 2, 3):
        zz = zat(r)
        vzs[r] = vp[chunk(zz, x)] + vxr[zz]
        send(vzs.at[r], vzr.at[r], vec_zbase + r - 1, z_dev(r))
    g_out[...] = out_rs.total().T
    g_fc[...] = fc_rs.total()
    own = vp[chunk(z, x)] + vxr[z]
    for r in (1, 2, 3):
        wait_recv(vzr.at[r], vec_zbase + r - 1)
        own = own + vzr[r]
    vcs[...] = own
    for r in (1, 2, 3):
        send(vcs, vcr.at[c], vec_cbase + r - 1, c_dev(r))
    vcr[c] = own
    qkv_total = qkv_rs.total()
    for j in range(3):
        g_qkv[j] = qkv_total[:, j * Q : (j + 1) * Q]
    g_proj[...] = proj_rs.total().T
    for r in (1, 2, 3):
        wait_recv(vcr.at[(c + NC - r) % NC], vec_cbase + r - 1)
    vec_out[...] = vcr[0] + vcr[1] + vcr[2] + vcr[3]

    for copy in sends:
        copy.wait_send()
    for cond, copy in guarded:

        @pl.when(cond)
        def _():
            copy.wait_send()


def write_kernel(*refs):
    block, inp, qkv, proj, fc, outw, vecs = refs[:7]
    outs, sems = refs[7:22], refs[22]
    order = [block, inp, vecs.at[0:1], vecs.at[1:2], qkv, vecs.at[2:3], vecs.at[3:4], proj, vecs.at[4:5],
             vecs.at[5:6], vecs.at[6:7], fc, vecs.at[8:12], outw, vecs.at[7:8]]
    copies = [pltpu.make_async_copy(a, b, sems.at[i]) for i, (a, b) in enumerate(zip(order, outs))]
    for copy in copies:
        copy.start()
    for copy in copies:
        copy.wait()


def fused_body(
    block_input, segment_ids, ln1_gain, ln1_bias, qkv_weight, query_bias, value_bias, proj_weight, proj_bias,
    ln2_gain, ln2_bias, fc_weight, fc_bias, out_weight, out_bias, cotangent,
):
    vmem = pl.BlockSpec(memory_space=pltpu.VMEM)
    hbm = pl.BlockSpec(memory_space=pl.ANY)

    def buf(*shape, kind=BF16):
        return pltpu.VMEM(shape, kind)

    widths = (3 * Q, Q, U, U)
    scratch = [
        buf(T, D), pltpu.VMEM((1, S), jnp.int32), *[buf(1, W) for _ in range(8)], buf(4, W), pltpu.SemaphoreType.DMA((18,)),
        buf(NDP, VEC_ROWS, W), buf(D, 3 * Q), buf(Q, D), buf(D, U), buf(U, D),
        *[buf(S, D) for _ in range(4)], *[buf(D, S) for _ in range(4)],
        buf(S, Q), buf(S, Q), buf(S, Q), buf(S, Q), buf(HEADS_HERE, S, S, kind=F32), buf(S, S, kind=F32),
        buf(S, U), buf(S, U, kind=F32), buf(S, U), buf(S, Q), buf(S, 3 * Q),
        buf(T, D, kind=F32), buf(T, D, kind=F32), buf(T, 1, kind=F32), buf(T, D, kind=F32), buf(T, 1, kind=F32),
        buf(T, D, kind=F32),
        *[buf(S, D) for _ in range(4)], *[buf(NC, T, D) for _ in range(4)],
        *[buf(NZ, W, n) for _ in range(4) for n in widths],
        buf(NDP, VEC_ROWS, W, kind=F32), buf(NZ, VEC_ROWS, W, kind=F32), buf(NZ, VEC_ROWS, W, kind=F32),
        buf(NZ, VEC_ROWS, W, kind=F32), buf(VEC_ROWS, W, kind=F32), buf(NC, VEC_ROWS, W, kind=F32),
        pltpu.SemaphoreType.DMA((144,)), pltpu.SemaphoreType.DMA((144,)),
    ]
    outs = pl.pallas_call(
        fused_kernel,
        out_shape=[
            jax.ShapeDtypeStruct((T, D), BF16),
            jax.ShapeDtypeStruct((T, D), F32),
            jax.ShapeDtypeStruct((3, W, Q), F32),
            jax.ShapeDtypeStruct((Q, W), F32),
            jax.ShapeDtypeStruct((W, U), F32),
            jax.ShapeDtypeStruct((U, W), F32),
            jax.ShapeDtypeStruct((VEC_ROWS, W), F32),
        ],
        in_specs=[hbm] * 16,
        out_specs=[vmem] * 7,
        scratch_shapes=scratch,
        compiler_params=pltpu.CompilerParams(
            collective_id=0, has_side_effects=True, vmem_limit_bytes=60 * 1024 * 1024
        ),
    )(
        block_input[0], cotangent[0], segment_ids, qkv_weight.transpose(1, 0, 2), proj_weight, fc_weight, out_weight,
        *[v.reshape(-1, W) for v in
          (ln1_gain, ln1_bias, query_bias, value_bias, proj_bias, ln2_gain, ln2_bias, out_bias, fc_bias)],
    )
    row = jax.ShapeDtypeStruct((1, W), F32)
    whole = [jax.ShapeDtypeStruct(o.shape, o.dtype) for o in outs[:6]]
    results = pl.pallas_call(
        write_kernel,
        out_shape=[whole[0], whole[1], row, row, whole[2], row, row, whole[3], row, row, row, whole[4],
                   jax.ShapeDtypeStruct((4, W), F32), whole[5], row],
        in_specs=[vmem] * 7,
        out_specs=[hbm] * 15,
        scratch_shapes=[pltpu.SemaphoreType.DMA((15,))],
    )(*outs)
    flat = (2, 3, 5, 6, 8, 9, 10, 12, 14)
    return tuple(r.reshape(-1) if i in flat else r[None] if i < 2 else r.transpose(1, 0, 2) if i == 4 else r for i, r in enumerate(results))


def solution(mesh):
    return jax.shard_map(
        fused_body if fits(mesh) else body,
        mesh=mesh,
        in_specs=(
            P("dp", "ctx", None),
            P("dp", None),
            P("dp"),
            P("dp"),
            P("dp", None, "ctx"),
            P("dp"),
            P("dp"),
            P("ctx", "dp"),
            P("dp"),
            P("dp"),
            P("dp"),
            P("dp", "ctx"),
            P("dp"),
            P("ctx", "dp"),
            P("dp"),
            P("dp", "ctx", None),
        ),
        out_specs=(
            P("dp", "ctx", None),
            P("dp", "ctx", None),
            P("dp"),
            P("dp"),
            P("dp", None, "ctx"),
            P("dp"),
            P("dp"),
            P("ctx", "dp"),
            P("dp"),
            P("dp"),
            P("dp"),
            P("dp", "ctx"),
            P("dp"),
            P("ctx", "dp"),
            P("dp"),
        ),
        check_vma=False,
    )
```

```python
import functools
import jax
import jax.numpy as jnp
from jax import lax
from jax.experimental import pallas as pl
from jax.experimental.pallas import tpu as pltpu
from jax.sharding import PartitionSpec as P

D = 1024
HD = 64
FF = 4096


NORM_EPS = 1e-05
GELU_ROOT = 0.7978845608028654
GELU_CUBE = 0.044715
MASK_VALUE = -1e30


def norm_forward(residual):
    row_mean = jnp.mean(residual, axis=-1, keepdims=True)
    centered = residual - row_mean
    row_var = jnp.mean(centered * centered, axis=-1, keepdims=True)
    inv_std = lax.rsqrt(row_var + NORM_EPS)
    return (centered * inv_std, inv_std)


def norm_backward(grad_in, normed, inv_std, gain):
    scaled = grad_in * gain
    mean_scaled = jnp.mean(scaled, axis=-1, keepdims=True)
    mean_cross = jnp.mean(scaled * normed, axis=-1, keepdims=True)
    return inv_std * (scaled - mean_scaled - normed * mean_cross)


def gelu_pair(pre_act):
    inner_arg = GELU_ROOT * (pre_act + GELU_CUBE * pre_act * pre_act * pre_act)
    tangent = jnp.tanh(inner_arg)
    activated = 0.5 * pre_act * (1.0 + tangent)
    gelu_slope = 0.5 * (1.0 + tangent) + 0.5 * pre_act * (1.0 - tangent * tangent) * GELU_ROOT * (
        1.0 + 3.0 * GELU_CUBE * pre_act * pre_act
    )
    return (activated, gelu_slope)


def masked_scores(query_heads, key_heads, allowed):
    raw_scores = jnp.einsum(
        "qhd,khd->hqk", query_heads, key_heads, preferred_element_type=jnp.float32
    ) * HD ** (-0.5)
    return jnp.where(allowed[None], raw_scores, MASK_VALUE)


def attend(query_heads, key_heads, value_heads, allowed):
    scores = masked_scores(query_heads, key_heads, allowed)
    top_score = jnp.max(scores, axis=-1, keepdims=True)
    log_total = top_score + jnp.log(jnp.sum(jnp.exp(scores - top_score), axis=-1, keepdims=True))
    attn_probs = jnp.where(allowed[None], jnp.exp(scores - log_total), 0.0)
    probs_half = attn_probs.astype(jnp.bfloat16)
    attended = jnp.einsum(
        "hqk,khd->qhd", probs_half, value_heads, preferred_element_type=jnp.float32
    )
    return (attended.reshape(query_heads.shape[0], -1).astype(jnp.bfloat16), log_total)


def attend_back(query_heads, key_heads, value_heads, allowed, log_total, grad_heads):
    scores = masked_scores(query_heads, key_heads, allowed)
    attn_probs = jnp.where(allowed[None], jnp.exp(scores - log_total), 0.0)
    probs_half = attn_probs.astype(jnp.bfloat16)
    prob_grad = jnp.einsum(
        "qhd,khd->hqk", grad_heads, value_heads, preferred_element_type=jnp.float32
    )
    value_part = jnp.einsum(
        "hqk,qhd->khd", probs_half, grad_heads, preferred_element_type=jnp.float32
    )
    delta_rows = jnp.sum(attn_probs * prob_grad, axis=-1, keepdims=True)
    score_grad = (attn_probs * (prob_grad - delta_rows) * HD ** (-0.5)).astype(jnp.bfloat16)
    query_grad = jnp.einsum(
        "hqk,khd->qhd", score_grad, key_heads, preferred_element_type=jnp.float32
    )
    key_part = jnp.einsum(
        "hqk,qhd->khd", score_grad, query_heads, preferred_element_type=jnp.float32
    )
    key_count = key_heads.shape[0]
    return (
        query_grad.reshape(query_heads.shape[0], -1),
        key_part.reshape(key_count, -1),
        value_part.reshape(key_count, -1),
    )


def place_part(part, whole_len, start):
    return lax.dynamic_update_slice_in_dim(jnp.zeros((whole_len,), jnp.float32), part, start, 0)


def body(
    block_input,
    segment_ids,
    ln1_gain,
    ln1_bias,
    qkv_weight,
    query_bias,
    value_bias,
    proj_weight,
    proj_bias,
    ln2_gain,
    ln2_bias,
    fc_weight,
    fc_bias,
    out_weight,
    out_bias,
    cotangent,
):
    tokens = block_input[0]
    seg_whole = segment_ids[0]
    grad_rows = cotangent[0]
    seq_length = seg_whole.shape[0]
    ctx_rank = lax.axis_index("ctx")
    key_pos = jnp.arange(seq_length, dtype=jnp.int32)
    resid_in = tokens.astype(jnp.float32)
    normed_one, inv_one = norm_forward(resid_in)
    grad_out = grad_rows.astype(jnp.float32)
    out_shift_grad = jnp.sum(grad_out, axis=0)
    vectors = lax.all_gather(
        jnp.concatenate(
            [ln1_gain, ln1_bias, query_bias, value_bias, proj_bias, ln2_gain, ln2_bias, out_bias, fc_bias]
        ),
        "dp",
        axis=0,
    )
    slice_len = ln1_gain.shape[0]
    dp_size = vectors.shape[0]
    ff_whole = fc_bias.shape[0] * dp_size

    def vector(at):
        return vectors[:, at * slice_len : (at + 1) * slice_len].astype(jnp.float32).reshape(-1)

    qkv_cols = lax.all_gather(qkv_weight, "dp", axis=0, tiled=True).reshape(D, -1)
    proj_rows = lax.all_gather(proj_weight, "dp", axis=1, tiled=True)
    fc_cols = lax.all_gather(fc_weight, "dp", axis=0, tiled=True)
    out_rows = lax.all_gather(out_weight, "dp", axis=1, tiled=True)
    quarter = proj_rows.shape[0]
    unit_part = fc_cols.shape[1]
    gain_first = vector(0)
    shift_first = vector(1)
    query_shift = lax.dynamic_slice_in_dim(vector(2), ctx_rank * quarter, quarter)
    value_shift = lax.dynamic_slice_in_dim(vector(3), ctx_rank * quarter, quarter)
    proj_shift = vector(4)
    gain_second = vector(5)
    shift_second = vector(6)
    out_shift = vector(7)
    fc_shift = lax.dynamic_slice_in_dim(
        vectors[:, 8 * slice_len :].astype(jnp.float32).reshape(-1), ctx_rank * unit_part, unit_part
    )
    local_heads = quarter // HD
    allowed = (key_pos[:, None] >= key_pos[None, :]) & (seg_whole[:, None] == seg_whole[None, :])
    hidden_one = (normed_one * gain_first + shift_first).astype(jnp.bfloat16)
    hidden_all, grad_all = (
        lax.all_gather(hidden_one, "ctx", axis=0, tiled=True),
        lax.all_gather(grad_rows, "ctx", axis=0, tiled=True),
    )
    qkv_out = jnp.dot(hidden_all, qkv_cols, preferred_element_type=jnp.float32)
    queries = (qkv_out[:, :quarter] + query_shift).astype(jnp.bfloat16)
    keys_here = qkv_out[:, quarter : 2 * quarter].astype(jnp.bfloat16)
    values_here = (qkv_out[:, 2 * quarter :] + value_shift).astype(jnp.bfloat16)
    query_heads = queries.reshape(seq_length, local_heads, HD)
    key_heads = keys_here.reshape(seq_length, local_heads, HD)
    value_heads = values_here.reshape(seq_length, local_heads, HD)
    attended, log_total = attend(query_heads, key_heads, value_heads, allowed)
    resid_mid = (
        resid_in
        + lax.psum_scatter(
            jnp.dot(attended, proj_rows, preferred_element_type=jnp.float32).astype(jnp.bfloat16),
            "ctx",
            scatter_dimension=0,
            tiled=True,
        ).astype(jnp.float32)
        + proj_shift
    )
    normed_two, inv_two = norm_forward(resid_mid)
    hidden_two = (normed_two * gain_second + shift_second).astype(jnp.bfloat16)
    hidden_two_all = lax.all_gather(hidden_two, "ctx", axis=0, tiled=True)
    pre_act = jnp.dot(hidden_two_all, fc_cols, preferred_element_type=jnp.float32) + fc_shift
    activated, gelu_slope = gelu_pair(pre_act)
    activated = activated.astype(jnp.bfloat16)
    block_output = (
        resid_mid
        + lax.psum_scatter(
            jnp.dot(activated, out_rows, preferred_element_type=jnp.float32).astype(jnp.bfloat16),
            "ctx",
            scatter_dimension=0,
            tiled=True,
        ).astype(jnp.float32)
        + out_shift
    ).astype(jnp.bfloat16)
    out_weight_grad = jnp.dot(activated.T, grad_all, preferred_element_type=jnp.float32)
    pre_grad = jnp.dot(grad_all, out_rows.T, preferred_element_type=jnp.float32) * gelu_slope
    fc_shift_grad = place_part(jnp.sum(pre_grad, axis=0), ff_whole, ctx_rank * unit_part)
    pre_grad_half = pre_grad.astype(jnp.bfloat16)
    fc_weight_grad = jnp.dot(hidden_two_all.T, pre_grad_half, preferred_element_type=jnp.float32)
    hidden_two_grad = lax.psum_scatter(
        jnp.dot(pre_grad_half, fc_cols.T, preferred_element_type=jnp.float32).astype(jnp.bfloat16),
        "ctx",
        scatter_dimension=0,
        tiled=True,
    ).astype(jnp.float32)
    gain_second_grad = jnp.sum(hidden_two_grad * normed_two, axis=0)
    shift_second_grad = jnp.sum(hidden_two_grad, axis=0)
    mid_grad = grad_out + norm_backward(hidden_two_grad, normed_two, inv_two, gain_second)
    proj_shift_grad = jnp.sum(mid_grad, axis=0)
    mid_grad_half = mid_grad.astype(jnp.bfloat16)
    mid_all = lax.all_gather(mid_grad_half, "ctx", axis=0, tiled=True)
    proj_weight_grad = jnp.dot(attended.T, mid_all, preferred_element_type=jnp.float32)
    attended_grad = jnp.dot(mid_all, proj_rows.T, preferred_element_type=jnp.float32).astype(
        jnp.bfloat16
    )
    grad_heads = attended_grad.reshape(seq_length, local_heads, HD)
    query_grad, key_grad, value_grad = attend_back(
        query_heads, key_heads, value_heads, allowed, log_total, grad_heads
    )
    query_shift_grad = place_part(jnp.sum(query_grad, axis=0), D, ctx_rank * quarter)
    value_shift_grad = place_part(jnp.sum(value_grad, axis=0), D, ctx_rank * quarter)
    qkv_grad = jnp.concatenate([query_grad, key_grad, value_grad], axis=1).astype(jnp.bfloat16)
    qkv_weight_grad = jnp.dot(hidden_all.T, qkv_grad, preferred_element_type=jnp.float32).reshape(
        D, 3, quarter
    )
    hidden_one_grad = lax.psum_scatter(
        jnp.dot(qkv_grad, qkv_cols.T, preferred_element_type=jnp.float32).astype(jnp.bfloat16),
        "ctx",
        scatter_dimension=0,
        tiled=True,
    ).astype(jnp.float32)
    gain_first_grad = jnp.sum(hidden_one_grad * normed_one, axis=0)
    shift_first_grad = jnp.sum(hidden_one_grad, axis=0)
    input_grad = mid_grad + norm_backward(hidden_one_grad, normed_one, inv_one, gain_first)
    half = jnp.bfloat16
    matrix_sums = (
        lax.psum_scatter(qkv_weight_grad.astype(half), "dp", scatter_dimension=0, tiled=True),
        lax.psum_scatter(proj_weight_grad.astype(half), "dp", scatter_dimension=1, tiled=True),
        lax.psum_scatter(fc_weight_grad.astype(half), "dp", scatter_dimension=0, tiled=True),
        lax.psum_scatter(out_weight_grad.astype(half), "dp", scatter_dimension=1, tiled=True),
    )
    matrix_sums = tuple(m.astype(jnp.float32) for m in matrix_sums)
    packed = jnp.concatenate(
        [
            v.reshape(dp_size, -1)
            for v in (
                gain_first_grad,
                shift_first_grad,
                query_shift_grad,
                value_shift_grad,
                proj_shift_grad,
                gain_second_grad,
                shift_second_grad,
                out_shift_grad,
                fc_shift_grad,
            )
        ],
        axis=1,
    )
    packed = lax.psum(packed, ("dp", "ctx"))
    mine = lax.dynamic_index_in_dim(packed, lax.axis_index("dp"), 0, keepdims=False)
    order = (0, 1, 2, 3, 4, 5, 6, 8, 7)
    pieces = [mine[i * slice_len : (i + 1) * slice_len] for i in range(8)] + [mine[8 * slice_len :]]
    vector_sums = tuple(pieces[i] for i in order)
    return (
        block_output[None],
        input_grad[None],
        vector_sums[0],
        vector_sums[1],
        matrix_sums[0],
        vector_sums[2],
        vector_sums[3],
        matrix_sums[1],
        vector_sums[4],
        vector_sums[5],
        vector_sums[6],
        matrix_sums[2],
        vector_sums[7],
        matrix_sums[3],
        vector_sums[8],
    )


NX = 2
NZ = 4
NDP = NX * NZ
NC = 4
T = 128
S = NC * T
W = 128
Q = D // NC
U = FF // NC
HEADS_HERE = Q // HD
BLK = 256
MESH = pl.DeviceIdType.MESH
F32 = jnp.float32
BF16 = jnp.bfloat16
VEC_ROWS = 16
UA = U // 2


def fits(mesh):
    return mesh.shape["dp"] == NDP and mesh.shape["ctx"] == NC


def dot(a, b):
    return jnp.dot(a, b, preferred_element_type=F32)


def dot_nt(a, b):
    return lax.dot_general(a, b, (((1,), (1,)), ((), ())), preferred_element_type=F32)


def dot_tn(a, b):
    return lax.dot_general(a, b, (((0,), (0,)), ((), ())), preferred_element_type=F32)


def fused_kernel(
    x_hbm, cot_hbm, seg_hbm, qkv_hbm, proj_hbm, fc_hbm, outw_hbm,
    v0, v1, v2, v3, v4, v5, v6, v7, v8,
    block_out, input_grad_out, g_qkv, g_proj, g_fc, g_out, vec_out,
    x_ref, seg_ref, n0, n1, n2, n3, n4, n5, n6, n7, n8, lsem,
    vec_g, qkv_g, proj_g, fc_g, out_g,
    h_all, cot_all, h2_all, mid_all, xt_h, xt_cot, xt_h2, xt_mid,
    q_s, k_s, v_s, att_s, p_s, bias_s, act_s, slope_s, pgh_s, ag_s, dqkv_s,
    resid_s, normed1_s, inv1_s, normed2_s, inv2_s, midg_s,
    rs_a, rs_b, rs_c, rs_d, rr_a, rr_b, rr_c, rr_d,
    xs_qkv, xs_proj, xs_fc, xs_out, xs_outb, xr_qkv, xr_proj, xr_fc, xr_out, xr_outb,
    zs_qkv, zs_proj, zs_fc, zs_out, zs_outb, zr_qkv, zr_proj, zr_fc, zr_out, zr_outb,
    vp, vxr, vzs, vzr, vcs, vcr,
    ssem, rsem,
):
    dp = lax.axis_index("dp")
    c = lax.axis_index("ctx")
    z = dp // NX
    x = dp % NX
    xo = 1 - x

    def zat(r):
        return (z + r) % NZ

    def chunk(zz, xx):
        return zz * NX + xx

    def span(i, n):
        return pl.ds(pl.multiple_of(i * n, n), n)

    counter = [0]
    sends = []
    guarded = []

    def sem_block(n):
        base = counter[0]
        counter[0] += n
        return base

    def remote(src, dst, sem, dev):
        return pltpu.make_async_remote_copy(
            src_ref=src, dst_ref=dst, send_sem=ssem.at[sem], recv_sem=rsem.at[sem],
            device_id=dev, device_id_type=MESH,
        )

    def send(src, dst, sem, dev):
        copy = remote(src, dst, sem, dev)
        copy.start()
        sends.append(copy)

    x_dev = (chunk(z, xo), c)

    def z_dev(r):
        return (chunk(zat(r), x), c)

    def c_dev(r):
        return (dp, (c + r) % NC)

    loads = []

    def load(src, dst):
        copy = pltpu.make_async_copy(src, dst, lsem.at[len(loads)])
        copy.start()
        loads.append(copy)

    def wait_recv(dst, sem):
        remote(dst, dst, sem, x_dev).wait_recv()

    def send_if(cond, src, dst, sem, dev):
        copy = remote(src, dst, sem, dev)

        @pl.when(cond)
        def _():
            copy.start()

        guarded.append((cond, copy))

    def z_next(up):
        return (chunk(z + 1 if up else z - 1, x), c)

    def has_next(up):
        return z < NZ - 1 if up else z > 0

    class Gather:
        def __init__(self, slot):
            self.slot = slot
            self.zbase, self.xbase = sem_block(2 * (NZ - 1)), sem_block(2 * (NZ - 1) + 1)

        def start_z(self):
            here = self.slot(dp)
            for up in (True, False):
                send_if(has_next(up), here, here, self.zbase + (0 if up else NZ - 1), z_next(up))

        def start_x(self):
            here = self.slot(dp)
            send(here, here, self.xbase + 2 * (NZ - 1), x_dev)

        def arrives(self, up, k):
            return (z >= k) if up else (z + k < NZ)

        def step(self, k):
            for up in (True, False):
                at = (0 if up else NZ - 1) + k - 1
                here = self.slot(chunk(z - k if up else z + k, x))

                @pl.when(self.arrives(up, k))
                def _():
                    wait_recv(here, self.zbase + at)

                if k < NZ - 1:
                    send_if(self.arrives(up, k) & has_next(up), here, here, self.zbase + at + 1, z_next(up))
                send_if(self.arrives(up, k), here, here, self.xbase + at, x_dev)

        def finish(self):
            wait_recv(self.slot(chunk(z, xo)), self.xbase + 2 * (NZ - 1))
            for k in range(1, NZ):
                for up in (True, False):

                    @pl.when(self.arrives(up, k))
                    def _():
                        wait_recv(
                            self.slot(chunk(z - k if up else z + k, xo)),
                            self.xbase + (0 if up else NZ - 1) + k - 1,
                        )

    class GatherXFirst:
        def __init__(self, slot):
            self.slot = slot
            self.zbase, self.xbase = sem_block(4 * (NZ - 1)), sem_block(1)

        def start_x(self):
            here = self.slot(dp)
            send(here, here, self.xbase, x_dev)

        def hop(self, here, sem, up, cond):
            send_if(cond, here, here, sem, z_next(up))

        def start_z(self):
            for col in (0, 1):
                if col:
                    wait_recv(self.slot(chunk(z, xo)), self.xbase)
                here = self.slot(chunk(z, xo if col else x))
                for up in (True, False):
                    self.hop(here, self.zbase + 6 * col + (0 if up else 3), up, has_next(up))

        def step(self, k):
            for col in (0, 1):
                for up in (True, False):
                    sem = self.zbase + 6 * col + (0 if up else 3) + k - 1
                    here = self.slot(chunk(z - k if up else z + k, xo if col else x))
                    cond = (z >= k) if up else (z + k < NZ)

                    @pl.when(cond)
                    def _():
                        wait_recv(here, sem)

                    if k < NZ - 1:
                        self.hop(here, sem + 1, up, cond & has_next(up))

    def rows_slot(buf):
        return lambda d: buf.at[span(d, W)]

    def cols_slot(buf):
        return lambda d: buf.at[:, span(d, W)]

    def part_slot(buf, lo, hi):
        return lambda d: buf.at[lo:hi, span(d, W)]

    vec_base = sem_block(NDP - 1)
    qkv_ag = Gather(rows_slot(qkv_g))
    proj_ag = Gather(cols_slot(proj_g))
    fc_ag = Gather(rows_slot(fc_g))
    out_ag = Gather(part_slot(out_g, 0, UA))
    outb_ag = GatherXFirst(part_slot(out_g, UA, U))

    mid = ((z + 1) // 2) % 2
    target = (3 * (1 - z // 2), (2 + 3 * z) % 5, 1 + z % 2)
    after = (z + 1 - 2 * (z // 2), z + 1 - 2 * (z % 2), z + 1 - 2 * (z // 2))
    lands = ((0, 1), (2, 3), (3, 4))

    class Reduce:
        def __init__(self, left, right, xs, xr, zs, zr, x_first=True):
            self.left, self.right, self.x_first = left, right, x_first
            self.xs, self.xr, self.zs, self.zr = xs, xr, zs, zr
            self.cols = (0,) if x_first else (0, 1)
            self.xbase, self.zbase = sem_block(NZ if x_first else 1), sem_block(5 * len(self.cols))

        def part(self, d):
            return dot(self.left[span(d, W), :], self.right[...])

        def pair(self, zz, col):
            got = self.part(chunk(zz, xo if col else x))
            if self.x_first:
                wait_recv(self.xr.at[zz], self.xbase + zz)
                got = got + self.xr[zz].astype(F32)
            return got

        def to_x(self):
            for zz in (*target, z):
                self.xs[zz] = self.part(chunk(zz, xo)).astype(BF16)
                send(self.xs.at[zz], self.xr.at[zz], self.xbase + zz, x_dev)

        def hop(self, i):
            for col in self.cols:
                base = self.zbase + 5 * col
                mine = self.pair(target[i], col)

                @pl.when(mid == 1)
                def _():
                    wait_recv(self.zr.at[5 * col + i], base + i)

                both = mine + self.zr[5 * col + i].astype(F32)
                self.zs[3 * col + i] = jnp.where(mid == 1, both, mine).astype(BF16)
                place = lands[i][0] + (lands[i][1] - lands[i][0]) * mid
                send(
                    self.zs.at[3 * col + i], self.zr.at[5 * col + place], base + place, (chunk(after[i], x), c)
                )

        def to_z(self):
            for i in range(3):
                self.hop(i)

        def column(self, col):
            own = self.pair(z, col)
            base = self.zbase + 5 * col
            wait_recv(self.zr.at[5 * col + 3], base + 3)
            own = own + self.zr[5 * col + 3].astype(F32)

            @pl.when(mid == 1)
            def _():
                wait_recv(self.zr.at[5 * col + 4], base + 4)

            return jnp.where(mid == 1, own + self.zr[5 * col + 4].astype(F32), own)

        def last_x(self):
            self.xs[0] = self.column(1).astype(BF16)
            send(self.xs.at[0], self.xr.at[0], self.xbase, x_dev)

        def total(self):
            own = self.column(0)
            if not self.x_first:
                wait_recv(self.xr.at[0], self.xbase)
                own = own + self.xr[0].astype(F32)
            return own

    out_rs = Reduce(xt_cot, act_s.at[:, :UA], xs_out, xr_out, zs_out, zr_out)
    outb_rs = Reduce(xt_cot, act_s.at[:, UA:], xs_outb, xr_outb, zs_outb, zr_outb, x_first=False)
    fc_rs = Reduce(xt_h2, pgh_s, xs_fc, xr_fc, zs_fc, zr_fc)
    proj_rs = Reduce(xt_mid, att_s, xs_proj, xr_proj, zs_proj, zr_proj)
    qkv_rs = Reduce(xt_h, dqkv_s, xs_qkv, xr_qkv, zs_qkv, zr_qkv)
    vec_xbase, vec_zbase, vec_cbase = sem_block(NZ), sem_block(NZ), sem_block(NC)

    class Share:
        def __init__(self, buf):
            self.buf, self.base = buf, sem_block(NC - 1)

        def start(self):
            here = self.buf.at[span(c, T)]
            for r in (2, 1, 3):
                send(here, here, self.base + r - 1, c_dev(r))

        def finish(self):
            for r in (1, 2, 3):
                wait_recv(self.buf.at[span((c + NC - r) % NC, T)], self.base + r - 1)

    class Scatter:
        def __init__(self, full, got):
            self.full, self.got, self.base = full, got, sem_block(NC - 1)

        def start(self):
            for r in (2, 1, 3):
                send(self.full.at[span((c + r) % NC, T)], self.got.at[r], self.base + r - 1, c_dev(r))

        def finish(self):
            total = self.full[span(c, T), :].astype(F32)
            for r in (1, 2, 3):
                wait_recv(self.got.at[r], self.base + r - 1)
                total = total + self.got[r].astype(F32)
            return total

    h_share, cot_share, h2_share, mid_share = Share(h_all), Share(cot_all), Share(h2_all), Share(mid_all)
    proj_sc, out_sc, h2g_sc, h1g_sc = (
        Scatter(rs_a, rr_a), Scatter(rs_b, rr_b), Scatter(rs_c, rr_c), Scatter(rs_d, rr_d)
    )

    vec_in = (n0, n1, n2, n3, n4, n5, n6, n7, n8)
    for src, dst in zip((v0, v1, v2, v3, v4, v5, v6, v7, v8), vec_in):
        load(src, dst)
    for j in range(3):
        load(qkv_hbm.at[j], qkv_g.at[span(dp, W), j * Q : (j + 1) * Q])
    load(proj_hbm, proj_g.at[:, span(dp, W)])
    load(x_hbm, x_ref)
    load(seg_hbm, seg_ref)
    load(cot_hbm, cot_all.at[span(c, T)])
    load(fc_hbm, fc_g.at[span(dp, W)])
    load(outw_hbm, out_g.at[:, span(dp, W)])
    barrier = pltpu.get_barrier_semaphore()
    peers = [((dp + r) % NDP, c) for r in range(1, NDP)] + [c_dev(r) for r in (1, 2, 3)]
    for dev in peers:
        pl.semaphore_signal(barrier, inc=1, device_id=dev, device_id_type=MESH)
    pl.semaphore_wait(barrier, len(peers))
    for copy in loads:
        copy.wait()
    vec_g[dp] = jnp.concatenate(
        [v[...].astype(F32) for v in vec_in] + [jnp.zeros((4, W), F32)], axis=0
    ).astype(BF16)
    for r in range(1, NDP):
        send(vec_g.at[dp], vec_g.at[dp], vec_base + r - 1, ((dp + r) % NDP, c))
    qkv_ag.start_z()
    qkv_ag.start_x()
    proj_ag.start_z()
    proj_ag.start_x()
    resid_in = x_ref[...].astype(F32)
    normed, inv = norm_forward(resid_in)
    normed1_s[...] = normed
    inv1_s[...] = inv
    key_pos = lax.broadcasted_iota(jnp.int32, (S, S), 1)
    query_pos = lax.broadcasted_iota(jnp.int32, (S, S), 0)
    seg_row = seg_ref[...].astype(F32)
    seg_down = jnp.broadcast_to(seg_row, (W, S)).T[:, :1]
    allowed = (query_pos >= key_pos) & (seg_down == seg_row)
    bias_s[...] = jnp.where(allowed, 0.0, MASK_VALUE)
    vp[...] = jnp.zeros_like(vp)

    for r in range(1, NDP):
        wait_recv(vec_g.at[(dp + NDP - r) % NDP], vec_base + r - 1)
    vectors = vec_g[...].astype(F32)

    def vector(row):
        return jnp.concatenate([vectors[d, row : row + 1, :] for d in range(NDP)], axis=1)

    gain1, shift1 = vector(0), vector(1)
    h_all[span(c, T), :] = (normed * gain1 + shift1).astype(BF16)
    h_share.start()
    cot_share.start()

    qkv_ag.step(1)
    qkv_ag.step(2)
    fc_ag.start_z()
    qkv_ag.step(3)
    fc_ag.start_x()
    for k in (1, 2, 3):
        proj_ag.step(k)
    fc_ag.step(1)
    outb_ag.start_x()
    out_ag.start_x()
    h_share.finish()
    qkv_ag.finish()
    def quarter_vector(row):
        first = vec_g[2 * c].astype(F32)[row : row + 1, :]
        second = vec_g[2 * c + 1].astype(F32)[row : row + 1, :]
        return jnp.concatenate([first, second], axis=1)

    q_s[...] = ((dot(h_all[...], qkv_g[:, :Q]) + quarter_vector(2)).astype(BF16).astype(F32) * HD ** (-0.5)).astype(BF16)
    k_s[...] = dot(h_all[...], qkv_g[:, Q : 2 * Q]).astype(BF16)
    v_s[...] = (dot(h_all[...], qkv_g[:, 2 * Q :]) + quarter_vector(3)).astype(BF16)


    fc_ag.step(2)
    out_ag.start_z()
    outb_ag.start_z()
    for h in range(HEADS_HERE):
        cols = slice(h * HD, (h + 1) * HD)
        for b in range(S // BLK):
            rows, upto = slice(b * BLK, (b + 1) * BLK), (b + 1) * BLK
            scores = dot_nt(q_s[rows, cols], k_s[:upto, cols]) + bias_s[rows, :upto]
            top = jnp.max(scores, axis=-1, keepdims=True)
            weights = jnp.exp(scores - top)
            probs = weights * (1.0 / jnp.sum(weights, axis=-1, keepdims=True))
            p_s[h, rows, :upto] = probs
            att_s[rows, cols] = dot(probs.astype(BF16), v_s[:upto, cols]).astype(BF16)

    fc_ag.step(3)
    proj_ag.finish()
    for i in range(D // 256):
        cols = slice(i * 256, (i + 1) * 256)
        rs_a[:, cols] = dot(att_s[...], proj_g[:, cols]).astype(BF16)
    proj_sc.start()
    xt_h[...] = h_all[...].T
    cot_share.finish()
    xt_cot[...] = cot_all[...].T
    out_ag.step(1)
    outb_ag.step(1)
    resid_mid = x_ref[...].astype(F32) + proj_sc.finish() + vector(4)
    resid_s[...] = resid_mid
    normed, inv = norm_forward(resid_mid)
    normed2_s[...] = normed
    inv2_s[...] = inv
    h2_all[span(c, T), :] = (normed * vector(5) + vector(6)).astype(BF16)
    h2_share.start()
    out_ag.step(2)
    outb_ag.step(2)
    h2_share.finish()
    fc_ag.finish()

    def fc_vector():
        pieces = []
        for i in range(2):
            block = vec_g[2 * c + i].astype(F32)
            pieces += [block[8 + k : 9 + k, :] for k in range(4)]
        return jnp.concatenate(pieces, axis=1)

    fc_shift = fc_vector()
    for i in range(U // 256):
        cols = slice(i * 256, (i + 1) * 256)
        activated, slope = gelu_pair(dot(h2_all[...], fc_g[:, cols]) + fc_shift[:, cols])
        act_s[:, cols] = activated.astype(BF16)
        slope_s[:, cols] = slope
    xt_h2[...] = h2_all[...].T

    out_ag.step(3)
    out_rs.to_x()
    outb_ag.step(3)
    outb_rs.hop(0)
    out_ag.finish()

    def put_quarter(row, total):
        for i in range(2):
            vp[2 * c + i, row : row + 1, :] = total[:, i * W : (i + 1) * W]

    def put_whole(row, total):
        for d in range(NDP):
            vp[d, row : row + 1, :] = total[:, d * W : (d + 1) * W]

    sums = []
    for i in range(U // 256):
        cols = slice(i * 256, (i + 1) * 256)
        pre_grad = dot_nt(cot_all[...], out_g[cols, :]) * slope_s[:, cols]
        sums.append(jnp.sum(pre_grad, axis=0, keepdims=True))
        pgh_s[:, cols] = pre_grad.astype(BF16)
    fc_sum = jnp.concatenate(sums, axis=1)
    for i in range(2):
        for k in range(4):
            at = i * 512 + k * W
            vp[2 * c + i, 8 + k : 9 + k, :] = fc_sum[:, at : at + W]

    for i in range(D // 256):
        cols = slice(i * 256, (i + 1) * 256)
        rs_c[:, cols] = dot_nt(pgh_s[...], fc_g[cols, :]).astype(BF16)
    h2g_sc.start()
    outb_rs.hop(1)
    fc_rs.to_x()
    for i in range(D // 256):
        cols = slice(i * 256, (i + 1) * 256)
        rs_b[:, cols] = dot(act_s[...], out_g[:, cols]).astype(BF16)

    grad_out = cot_all[span(c, T), :].astype(F32)
    h2_grad = h2g_sc.finish()
    mid_grad = grad_out + norm_backward(h2_grad, normed2_s[...], inv2_s[...], vector(5))
    mid_all[span(c, T), :] = mid_grad.astype(BF16)
    mid_share.start()
    out_sc.start()
    midg_s[...] = mid_grad
    put_whole(4, jnp.sum(mid_grad, axis=0, keepdims=True))
    put_whole(5, jnp.sum(h2_grad * normed2_s[...], axis=0, keepdims=True))
    put_whole(6, jnp.sum(h2_grad, axis=0, keepdims=True))
    put_whole(7, jnp.sum(grad_out, axis=0, keepdims=True))
    out_rs.hop(0)
    outb_rs.hop(2)
    out_rs.hop(1)
    mid_share.finish()
    ag_s[...] = dot_nt(mid_all[...], proj_g[...]).astype(BF16)

    out_rs.hop(2)
    xt_mid[...] = mid_all[...].T
    proj_rs.to_x()

    for h in range(HEADS_HERE):
        if h:
            fc_rs.hop(h - 1)
        cols = slice(h * HD, (h + 1) * HD)
        key_grad = [jnp.zeros((BLK, HD), F32) for _ in range(S // BLK)]
        value_grad = [jnp.zeros((BLK, HD), F32) for _ in range(S // BLK)]
        query_sum = jnp.zeros((1, HD), F32)
        for b in range(S // BLK):
            rows, upto = slice(b * BLK, (b + 1) * BLK), (b + 1) * BLK
            probs = p_s[h, rows, :upto]
            grads = ag_s[rows, cols]
            prob_grad = dot_nt(grads, v_s[:upto, cols])
            delta = jnp.sum(probs * prob_grad, axis=-1, keepdims=True)
            score_grad = (probs * (prob_grad - delta)).astype(BF16)
            half = probs.astype(BF16)
            query_grad = dot(score_grad, k_s[:upto, cols]) * HD ** (-0.5)
            query_sum = query_sum + jnp.sum(query_grad, axis=0, keepdims=True)
            dqkv_s[rows, h * HD : (h + 1) * HD] = query_grad.astype(BF16)
            key_part = dot_tn(score_grad, q_s[rows, cols])
            value_part = dot_tn(half, grads)
            for k in range(b + 1):
                key_grad[k] = key_grad[k] + key_part[k * BLK : (k + 1) * BLK, :]
                value_grad[k] = value_grad[k] + value_part[k * BLK : (k + 1) * BLK, :]
        value_sum = jnp.zeros((1, HD), F32)
        for k in range(S // BLK):
            rows = slice(k * BLK, (k + 1) * BLK)
            dqkv_s[rows, Q + h * HD : Q + (h + 1) * HD] = key_grad[k].astype(BF16)
            dqkv_s[rows, 2 * Q + h * HD : 2 * Q + (h + 1) * HD] = value_grad[k].astype(BF16)
            value_sum = value_sum + jnp.sum(value_grad[k], axis=0, keepdims=True)
        lane = slice((h % 2) * HD, (h % 2 + 1) * HD)
        vp[2 * c + h // 2, 2:3, lane] = query_sum
        vp[2 * c + h // 2, 3:4, lane] = value_sum

    for i in range(D // 256):
        cols = slice(i * 256, (i + 1) * 256)
        rs_d[:, cols] = dot_nt(dqkv_s[...], qkv_g[cols, :]).astype(BF16)
    h1g_sc.start()
    qkv_rs.to_x()
    proj_rs.to_z()

    h1_grad = h1g_sc.finish()
    put_whole(0, jnp.sum(h1_grad * normed1_s[...], axis=0, keepdims=True))
    put_whole(1, jnp.sum(h1_grad, axis=0, keepdims=True))
    for j in range(NZ):
        send(vp.at[chunk(j, xo)], vxr.at[j], vec_xbase + j, x_dev)
    input_grad_out[...] = midg_s[...] + norm_backward(h1_grad, normed1_s[...], inv1_s[...], gain1)
    block_out[...] = (resid_s[...] + out_sc.finish() + vector(7)).astype(BF16)

    qkv_rs.to_z()
    for j in range(NZ):
        wait_recv(vxr.at[j], vec_xbase + j)
    for r in (1, 2, 3):
        zz = zat(r)
        vzs[r] = vp[chunk(zz, x)] + vxr[zz]
        send(vzs.at[r], vzr.at[r], vec_zbase + r - 1, z_dev(r))
    g_out[:UA, :] = out_rs.total().T
    outb_rs.last_x()
    g_fc[...] = fc_rs.total()
    own = vp[chunk(z, x)] + vxr[z]
    for r in (1, 2, 3):
        wait_recv(vzr.at[r], vec_zbase + r - 1)
        own = own + vzr[r]
    vcs[...] = own
    for r in (1, 2, 3):
        send(vcs, vcr.at[c], vec_cbase + r - 1, c_dev(r))
    vcr[c] = own
    g_out[UA:, :] = outb_rs.total().T
    qkv_total = qkv_rs.total()
    for j in range(3):
        g_qkv[j] = qkv_total[:, j * Q : (j + 1) * Q]
    g_proj[...] = proj_rs.total().T
    for r in (1, 2, 3):
        wait_recv(vcr.at[(c + NC - r) % NC], vec_cbase + r - 1)
    vec_out[...] = vcr[0] + vcr[1] + vcr[2] + vcr[3]

    for copy in sends:
        copy.wait_send()
    for cond, copy in guarded:

        @pl.when(cond)
        def _():
            copy.wait_send()


def write_kernel(*refs):
    block, inp, qkv, proj, fc, outw, vecs = refs[:7]
    outs, sems = refs[7:22], refs[22]
    order = [block, inp, vecs.at[0:1], vecs.at[1:2], qkv, vecs.at[2:3], vecs.at[3:4], proj, vecs.at[4:5],
             vecs.at[5:6], vecs.at[6:7], fc, vecs.at[8:12], outw, vecs.at[7:8]]
    copies = [pltpu.make_async_copy(a, b, sems.at[i]) for i, (a, b) in enumerate(zip(order, outs))]
    for copy in copies:
        copy.start()
    for copy in copies:
        copy.wait()


def fused_body(
    block_input, segment_ids, ln1_gain, ln1_bias, qkv_weight, query_bias, value_bias, proj_weight, proj_bias,
    ln2_gain, ln2_bias, fc_weight, fc_bias, out_weight, out_bias, cotangent,
):
    vmem = pl.BlockSpec(memory_space=pltpu.VMEM)
    hbm = pl.BlockSpec(memory_space=pl.ANY)

    def buf(*shape, kind=BF16):
        return pltpu.VMEM(shape, kind)

    widths = (3 * Q, Q, U, UA, U - UA)
    scratch = [
        buf(T, D), pltpu.VMEM((1, S), jnp.int32), *[buf(1, W) for _ in range(8)], buf(4, W), pltpu.SemaphoreType.DMA((18,)),
        buf(NDP, VEC_ROWS, W), buf(D, 3 * Q), buf(Q, D), buf(D, U), buf(U, D),
        *[buf(S, D) for _ in range(4)], *[buf(D, S) for _ in range(4)],
        buf(S, Q), buf(S, Q), buf(S, Q), buf(S, Q), buf(HEADS_HERE, S, S, kind=F32), buf(S, S, kind=F32),
        buf(S, U), buf(S, U, kind=F32), buf(S, U), buf(S, Q), buf(S, 3 * Q),
        buf(T, D, kind=F32), buf(T, D, kind=F32), buf(T, 1, kind=F32), buf(T, D, kind=F32), buf(T, 1, kind=F32),
        buf(T, D, kind=F32),
        *[buf(S, D) for _ in range(4)], *[buf(NC, T, D) for _ in range(4)],
        *[buf(m, W, n) for ms in ((4, 4, 4, 4, 1), (4, 4, 4, 4, 1), (3, 3, 3, 3, 6), (5, 5, 5, 5, 10))
          for m, n in zip(ms, widths)],
        buf(NDP, VEC_ROWS, W, kind=F32), buf(NZ, VEC_ROWS, W, kind=F32), buf(NZ, VEC_ROWS, W, kind=F32),
        buf(NZ, VEC_ROWS, W, kind=F32), buf(VEC_ROWS, W, kind=F32), buf(NC, VEC_ROWS, W, kind=F32),
        pltpu.SemaphoreType.DMA((192,)), pltpu.SemaphoreType.DMA((192,)),
    ]
    outs = pl.pallas_call(
        fused_kernel,
        out_shape=[
            jax.ShapeDtypeStruct((T, D), BF16),
            jax.ShapeDtypeStruct((T, D), F32),
            jax.ShapeDtypeStruct((3, W, Q), F32),
            jax.ShapeDtypeStruct((Q, W), F32),
            jax.ShapeDtypeStruct((W, U), F32),
            jax.ShapeDtypeStruct((U, W), F32),
            jax.ShapeDtypeStruct((VEC_ROWS, W), F32),
        ],
        in_specs=[hbm] * 16,
        out_specs=[vmem] * 7,
        scratch_shapes=scratch,
        compiler_params=pltpu.CompilerParams(
            collective_id=0, has_side_effects=True, vmem_limit_bytes=60 * 1024 * 1024
        ),
    )(
        block_input[0], cotangent[0], segment_ids, qkv_weight.transpose(1, 0, 2), proj_weight, fc_weight, out_weight,
        *[v.reshape(-1, W) for v in
          (ln1_gain, ln1_bias, query_bias, value_bias, proj_bias, ln2_gain, ln2_bias, out_bias, fc_bias)],
    )
    row = jax.ShapeDtypeStruct((1, W), F32)
    whole = [jax.ShapeDtypeStruct(o.shape, o.dtype) for o in outs[:6]]
    results = pl.pallas_call(
        write_kernel,
        out_shape=[whole[0], whole[1], row, row, whole[2], row, row, whole[3], row, row, row, whole[4],
                   jax.ShapeDtypeStruct((4, W), F32), whole[5], row],
        in_specs=[vmem] * 7,
        out_specs=[hbm] * 15,
        scratch_shapes=[pltpu.SemaphoreType.DMA((15,))],
    )(*outs)
    flat = (2, 3, 5, 6, 8, 9, 10, 12, 14)
    return tuple(r.reshape(-1) if i in flat else r[None] if i < 2 else r.transpose(1, 0, 2) if i == 4 else r for i, r in enumerate(results))


def solution(mesh):
    return jax.shard_map(
        fused_body if fits(mesh) else body,
        mesh=mesh,
        in_specs=(
            P("dp", "ctx", None),
            P("dp", None),
            P("dp"),
            P("dp"),
            P("dp", None, "ctx"),
            P("dp"),
            P("dp"),
            P("ctx", "dp"),
            P("dp"),
            P("dp"),
            P("dp"),
            P("dp", "ctx"),
            P("dp"),
            P("ctx", "dp"),
            P("dp"),
            P("dp", "ctx", None),
        ),
        out_specs=(
            P("dp", "ctx", None),
            P("dp", "ctx", None),
            P("dp"),
            P("dp"),
            P("dp", None, "ctx"),
            P("dp"),
            P("dp"),
            P("ctx", "dp"),
            P("dp"),
            P("dp"),
            P("dp"),
            P("dp", "ctx"),
            P("dp"),
            P("ctx", "dp"),
            P("dp"),
        ),
        check_vma=False,
    )
```
